32 devices in a mesh: region: 4 (over z), tile: 8 (over y, x, core).
Axes of the slice: x: 2, y: 2, z: 4, core: 2. Of those that a mesh axis runs over, the one named last changes fastest.
Arguments:
- global_field: bfloat16 [70, 512, 1280], P(None, 'tile', 'region'), may hold values from -6 to 6
- regional_state: bfloat16 [32, 99, 64, 128], P(('region', 'tile')), may hold values from -6 to 6
- windows: int32 [8, 4], replicated, may hold values from 0 to 1152, as said below
- longitude_weights: bfloat16 [8, 512, 128], replicated, may hold values from -0.75 to 0.75
- latitude_weights: bfloat16 [8, 64, 64], P('region'), may hold values from -1 to 1
- first_kernel: bfloat16 [3, 3, 96, 169], replicated, may hold values from -0.15625 to 0.15625
- first_bias: float32 [96], replicated, may hold values from -3 to 3
- second_kernel: bfloat16 [3, 3, 96, 96], replicated, may hold values from -0.21875 to 0.21875
- later_conv_bias: float32 [96], replicated, may hold values from -3 to 3
- shortcut_weight: bfloat16 [96, 169], replicated, may hold values from -0.5 to 0.5
Outputs:
- block_output: bfloat16 [32, 96, 64, 128], P(('region', 'tile'))
The draws below stay inside these ranges and needn't reach their ends.
Inputs may be any that keep to these rules, and one draw needn't show every extreme that they name: `windows`: columns per domain: latitude start 0 to 448, latitude rows used 64 // 2 to 64, longitude start 0 to 1152, longitude columns used 128 // 2 to 128; some domain uses all 64 rows and some all 128 columns.
All inputs are finite; a program needn't handle non-finite values.
Results may differ from the reference program's by a relative error of at most 0.0053.
Values may be sent and summed in bfloat16 or wider, within the bound.
A program may use at most 128 MiB of HBM per device.

```python
import jax
import jax.numpy as jnp
from jax import lax

GCH = 70
SCH = 99
OCH = 96
TCOLS = 4
HY = 64
HX = 128
LAT = 512
LON = 1280
LWIN = 64
KWIN = 128
CIN = 169
DOMAINS = 8
TILES = 32
RY = 64
RX = 512
N_REGION = 4
N_TILE = 8


def draw_windows(key, part):
    subkeys = jax.random.split(key, 5)
    lat_start = jax.random.randint(subkeys[0], (DOMAINS,), 0, LAT - LWIN + 1)
    lat_count = jax.random.randint(subkeys[1], (DOMAINS,), LWIN // 2, LWIN + 1)
    lon_start = jax.random.randint(subkeys[2], (DOMAINS,), 0, LON - KWIN + 1)
    lon_count = jax.random.randint(subkeys[3], (DOMAINS,), KWIN // 2, KWIN + 1)
    fullest = jax.random.randint(subkeys[4], (2,), 0, DOMAINS)
    domain_slots = jnp.arange(DOMAINS)
    lat_count = jnp.where(domain_slots == fullest[0], LWIN, lat_count)
    lon_count = jnp.where(domain_slots == fullest[1], KWIN, lon_count)
    return jnp.stack([lat_start, lat_count, lon_start, lon_count], axis=1).astype(jnp.int32)


def shard_levels(own_key, dims, cuts, low, high):
    def one(axis_at, parts):
        heights = jax.random.uniform(jax.random.fold_in(jax.random.fold_in(own_key, 6), axis_at), (parts,), jnp.float32, low / len(cuts), high / len(cuts))
        return jnp.repeat(jnp.exp(heights), dims[axis_at] // parts).reshape((-1,) + (1,) * (len(dims) - axis_at - 1))

    level = one(*cuts[0])
    for cut in cuts[1:]:
        level = level * one(*cut)
    return level


def scatter_about(own_key, extent, scale, limit, pieces=(), kind=jnp.bfloat16):
    factor_of = shard_levels(own_key, extent, pieces, -0.22, 0.18) if pieces else 1.0
    result = jax.random.normal(own_key, extent, jnp.float32) * scale * factor_of
    return jnp.minimum(jnp.maximum(result, -limit), limit).astype(kind)


def setup_inputs(seed: int = 0) -> dict:
    splits = jax.random.split(jax.random.key(seed), 11)
    global_field = scatter_about(splits[0], (GCH, LAT, LON), 1.0, 6.0, ((1, 8), (2, 4)))
    regional_state = scatter_about(splits[1], (TILES, SCH, HY, HX), 1.0, 6.0, ((0, 32),))
    windows = draw_windows(jax.random.fold_in(splits[10], 71), 0)
    longitude_weights = scatter_about(splits[3], (DOMAINS, RX, KWIN), (KWIN // 2) ** -0.5, 0.75)
    latitude_weights = scatter_about(splits[4], (DOMAINS, RY, LWIN), (LWIN // 2) ** -0.5, 1.0, ((0, 4),))
    first_kernel = scatter_about(splits[5], (3, 3, OCH, CIN), (9 * CIN) ** -0.5, 0.15625)
    first_bias = scatter_about(splits[6], (OCH,), 0.5, 3.0, (), jnp.float32)
    second_kernel = scatter_about(splits[7], (3, 3, OCH, OCH), (9 * OCH) ** -0.5, 0.21875)
    later_conv_bias = scatter_about(splits[8], (OCH,), 0.5, 3.0, (), jnp.float32)
    shortcut_weight = scatter_about(splits[9], (OCH, CIN), CIN ** -0.5, 0.5)
    return {"global_field": global_field, "regional_state": regional_state, "windows": windows, "longitude_weights": longitude_weights, "latitude_weights": latitude_weights, "first_kernel": first_kernel, "first_bias": first_bias, "second_kernel": second_kernel, "later_conv_bias": later_conv_bias, "shortcut_weight": shortcut_weight}


def domain_field(tiles, domain):
    per_domain = N_TILE // 2
    tile_rows_count = per_domain // TCOLS
    block = tiles[domain * per_domain:(domain + 1) * per_domain]
    channels = block.shape[1]
    block = block.reshape(tile_rows_count, TCOLS, channels, HY, HX).transpose(2, 0, 3, 1, 4)
    return block.reshape(channels, tile_rows_count * HY, TCOLS * HX)


def field_tiles(field):
    per_domain = N_TILE // 2
    tile_rows_count = per_domain // TCOLS
    channels = field.shape[0]
    block = field.reshape(channels, tile_rows_count, HY, TCOLS, HX).transpose(1, 3, 0, 2, 4)
    return block.reshape(per_domain, channels, HY, HX)


def convolve(padded, kernel, out_rows, out_cols):
    total = jnp.zeros((kernel.shape[2], out_rows, out_cols), jnp.float32)
    for vertical in range(3):
        for lateral in range(3):
            window = padded[:, vertical:vertical + out_rows, lateral:lateral + out_cols].astype(jnp.float32)
            total = total + jnp.einsum("oc,chw->ohw", kernel[vertical, lateral].astype(jnp.float32), window)
    return total


def reference(global_field, regional_state, windows, longitude_weights, latitude_weights, first_kernel, first_bias, second_kernel, later_conv_bias, shortcut_weight):
    rotation = N_TILE // 4 + 2
    groups = []
    for group in range(N_REGION):
        groups.append(jnp.roll(regional_state[group * N_TILE:(group + 1) * N_TILE], rotation, axis=0))
    arranged = jnp.concatenate(groups, axis=0)
    results = []
    for domain in range(DOMAINS):
        lat_start = windows[domain, 0]
        lat_count = windows[domain, 1]
        lon_start = windows[domain, 2]
        lon_count = windows[domain, 3]
        longitude_matrix = longitude_weights[domain].astype(jnp.float32) * (jnp.arange(KWIN) < lon_count).astype(jnp.float32)[None, :]
        lat_mat = latitude_weights[domain].astype(jnp.float32) * (jnp.arange(LWIN) < lat_count).astype(jnp.float32)[None, :]
        incoming_field = lax.dynamic_slice_in_dim(global_field, lon_start, KWIN, 2).astype(jnp.float32)
        latitude_strips = jnp.einsum("yep,bp->yeb", incoming_field, longitude_matrix).astype(jnp.bfloat16)
        picked = lax.dynamic_slice_in_dim(latitude_strips, lat_start, LWIN, 1).astype(jnp.float32)
        condition = jnp.einsum("yl,clx->cyx", lat_mat, picked).astype(jnp.bfloat16)
        inputs = jnp.concatenate([domain_field(arranged, domain), condition], axis=0)
        total_row_count = inputs.shape[1]
        cols_total = inputs.shape[2]
        padded = jnp.pad(inputs, ((0, 0), (1, 1), (1, 1)))
        first = convolve(padded, first_kernel, total_row_count, cols_total) + first_bias[:, None, None]
        hidden = jax.nn.silu(first).astype(jnp.bfloat16)
        padded_hidden = jnp.pad(hidden, ((0, 0), (1, 1), (1, 1)))
        second = convolve(padded_hidden, second_kernel, total_row_count, cols_total) + later_conv_bias[:, None, None]
        skipped = jnp.einsum("oc,chw->ohw", shortcut_weight.astype(jnp.float32), inputs.astype(jnp.float32))
        output = (second + skipped).astype(jnp.bfloat16)
        results.append(field_tiles(output))
    placed = jnp.concatenate(results, axis=0)
    outputs = []
    for group in range(N_REGION):
        outputs.append(jnp.roll(placed[group * N_TILE:(group + 1) * N_TILE], -rotation, axis=0))
    return jnp.concatenate(outputs, axis=0)
```

```python
import jax
import jax.numpy as jnp
from jax import lax
from jax.sharding import PartitionSpec as P

TCOLS = 4
BF = jnp.bfloat16
F32 = jnp.float32


def passed_along(block, axis, distance):
    devices = range(lax.axis_size(axis))
    route = [((i - distance) % len(devices), i) for i in devices]
    return lax.ppermute(block, axis, route)


def windows_of_domains(field, windows, region_index, lat_window, lon_window):
    tiles = lax.axis_size("tile")
    channels, band, cols = field.shape
    share = -(-channels // tiles)
    padded = jnp.pad(field, ((0, share * tiles - channels), (0, 0), (0, 0)))
    split = padded.reshape(tiles, share, band, cols)
    bands = lax.all_to_all(split, "tile", split_axis=0, concat_axis=0, tiled=True)
    per = lat_window // band
    groups = bands.reshape(tiles // per, per, share, band, cols)
    groups = groups.transpose(0, 2, 1, 3, 4).reshape(tiles // per, share, lat_window, cols)
    count = groups.shape[0]
    row = jnp.arange(lat_window)[None, :, None]
    col = jnp.arange(cols)[:, None] + region_index * cols
    pieces = []
    for domain in range(windows.shape[0]):
        group, shift = windows[domain, 0] // lat_window, windows[domain, 0] % lat_window
        here = lax.dynamic_index_in_dim(groups, group, 0, keepdims=False)
        following = lax.dynamic_index_in_dim(groups, jnp.minimum(group + 1, count - 1), 0, keepdims=False)
        rows = jnp.where(row >= shift, here, following)
        pick = (col == jnp.arange(lon_window)[None, :] + windows[domain, 2]).astype(BF)
        pieces.append(jnp.einsum("clj,jk->clk", rows, pick, preferred_element_type=F32).astype(BF))
    return jnp.stack(pieces)


def shards(
    global_field,
    regional_state,
    windows,
    longitude_weights,
    latitude_weights,
    first_kernel,
    first_bias,
    second_kernel,
    later_conv_bias,
    shortcut_weight,
):
    tiles = lax.axis_size("tile")
    regions = lax.axis_size("region")
    tile_index = lax.axis_index("tile")
    region_index = lax.axis_index("region")
    half = tiles // 2
    row_tiles = half // TCOLS
    rotation = tiles // 4 + 2
    position = (tile_index + rotation) % tiles
    domain_half = position // half
    within = position % half
    row_tile = within // TCOLS
    col_tile = within % TCOLS
    my_domain = 2 * region_index + domain_half
    state = regional_state[0]
    channels, rows, cols = state.shape
    field_channels = global_field.shape[0]

    pieces = windows_of_domains(
        global_field, windows, region_index, latitude_weights.shape[2], longitude_weights.shape[2]
    )
    share = pieces.shape[1]
    sent = pieces.reshape((regions, 2) + pieces.shape[1:])
    got = lax.all_to_all(sent, "region", split_axis=0, concat_axis=0, tiled=True)
    mine = got.astype(F32).sum(0).astype(BF)
    halves = [((t + rotation) % tiles) // half for t in range(tiles)]
    spread = jnp.stack([mine[h] for h in halves])
    window = lax.all_to_all(spread, "tile", split_axis=0, concat_axis=0, tiled=True)
    window = window.reshape((tiles * share,) + window.shape[2:])[:field_channels]

    own = lax.dynamic_index_in_dim(windows, my_domain, 0, keepdims=False)
    lon = lax.dynamic_index_in_dim(longitude_weights, my_domain, 0, keepdims=False)
    lon = lon * (jnp.arange(lon.shape[1]) < own[3]).astype(BF)[None, :]
    lon = lax.dynamic_slice_in_dim(jnp.pad(lon, ((2, 2), (0, 0))), col_tile * cols, cols + 4, 0)
    lat = lax.dynamic_index_in_dim(latitude_weights, domain_half, 0, keepdims=False)
    lat = lat * (jnp.arange(lat.shape[1]) < own[1]).astype(BF)[None, :]
    lat = lax.dynamic_slice_in_dim(jnp.pad(lat, ((2, 2), (0, 0))), row_tile * rows, rows + 4, 0)
    lat = jnp.roll(lat, own[0] % lat.shape[1], axis=1)

    bands = jnp.einsum("clk,xk->clx", window, lon, preferred_element_type=F32).astype(BF)
    condition = jnp.einsum("yl,clx->cyx", lat, bands, preferred_element_type=F32).astype(BF)

    left = passed_along(state[:, :, cols - 2 :], "tile", 1) * (col_tile > 0).astype(BF)
    right = passed_along(state[:, :, :2], "tile", -1) * (col_tile < TCOLS - 1).astype(BF)
    wide = jnp.concatenate([left, state, right], axis=2)
    if row_tiles > 1:
        above = passed_along(wide[:, rows - 2 :, :], "tile", TCOLS) * (row_tile > 0).astype(BF)
        below = passed_along(wide[:, :2, :], "tile", -TCOLS) * (row_tile < row_tiles - 1).astype(BF)
        wide = jnp.concatenate([above, wide, below], axis=1)
    else:
        wide = jnp.pad(wide, ((0, 0), (2, 2), (0, 0)))

    def conv(value, kernel):
        return lax.conv_general_dilated(
            value[None], kernel, (1, 1), "VALID", dimension_numbers=("NCHW", "HWOI", "NCHW"),
            preferred_element_type=F32,
        )[0]

    inputs = jnp.concatenate([wide, condition], axis=0)
    first = conv(inputs, first_kernel) + first_bias[:, None, None]
    hidden = jax.nn.silu(first).astype(BF)
    y = jnp.arange(rows + 2) - 1 + row_tile * rows
    x = jnp.arange(cols + 2) - 1 + col_tile * cols
    inside = ((y >= 0) & (y < row_tiles * rows))[:, None] & ((x >= 0) & (x < TCOLS * cols))[None, :]
    hidden = jnp.where(inside[None], hidden, jnp.zeros((), BF))
    second = conv(hidden, second_kernel) + later_conv_bias[:, None, None]
    core = inputs[:, 2:-2, 2:-2]
    skipped = jnp.einsum("oc,chw->ohw", shortcut_weight, core, preferred_element_type=F32)
    return (second + skipped)[None].astype(BF)


def solution(mesh):
    placed = (
        P(None, "tile", "region"),
        P(("region", "tile"), None, None, None),
        P(),
        P(),
        P("region", None, None),
        P(),
        P(),
        P(),
        P(),
        P(),
    )
    return jax.shard_map(
        shards,
        mesh=mesh,
        in_specs=placed,
        out_specs=P(("region", "tile"), None, None, None),
        check_vma=False,
    )
```

```python
import functools

import jax
import jax.numpy as jnp
from jax import lax
from jax.experimental import pallas as pl
from jax.experimental.pallas import tpu as pltpu
from jax.sharding import PartitionSpec as P

TCOLS = 4
BF = jnp.bfloat16
F32 = jnp.float32


def passed_along(block, axis, distance):
    devices = range(lax.axis_size(axis))
    route = [((i - distance) % len(devices), i) for i in devices]
    return lax.ppermute(block, axis, route)


def windows_of_domains(field, windows, region_index, lat_window, lon_window):
    tiles = lax.axis_size("tile")
    channels, band, cols = field.shape
    share = -(-channels // tiles)
    padded = jnp.pad(field, ((0, share * tiles - channels), (0, 0), (0, 0)))
    split = padded.reshape(tiles, share, band, cols)
    bands = lax.all_to_all(split, "tile", split_axis=0, concat_axis=0, tiled=True)
    per = lat_window // band
    groups = bands.reshape(tiles // per, per, share, band, cols)
    groups = groups.transpose(0, 2, 1, 3, 4).reshape(tiles // per, share, lat_window, cols)
    count = groups.shape[0]
    row = jnp.arange(lat_window)[None, :, None]
    col = jnp.arange(cols)[:, None] + region_index * cols
    pieces = []
    for domain in range(windows.shape[0]):
        group, shift = windows[domain, 0] // lat_window, windows[domain, 0] % lat_window
        here = lax.dynamic_index_in_dim(groups, group, 0, keepdims=False)
        following = lax.dynamic_index_in_dim(groups, jnp.minimum(group + 1, count - 1), 0, keepdims=False)
        rows = jnp.where(row >= shift, here, following)
        pick = (col == jnp.arange(lon_window)[None, :] + windows[domain, 2]).astype(BF)
        pieces.append(jnp.einsum("clj,jk->clk", rows, pick, preferred_element_type=F32).astype(BF))
    return jnp.stack(pieces)


def around(value, lanes):
    zeros = jnp.zeros(value.shape[:-1] + (lanes - value.shape[-1],), value.dtype)
    return jnp.concatenate([value[..., 2:], zeros, value[..., :2]], axis=-1)


def with_neighbours(value):
    return jnp.concatenate([pltpu.roll(value, 1, 1), value, pltpu.roll(value, value.shape[1] - 1, 1)], axis=0)


def block_kernel(step_rows, out, place, mask_ref, state_ref, cond_ref, w1_ref, b1_ref, w2_ref, b2_ref, o_ref, a1, c1, a2, c2):
    step = pl.program_id(0)

    @pl.when(step == 0)
    def _():
        for ref in (a1, c1, a2, c2):
            ref[...] = jnp.zeros_like(ref)

    width = o_ref.shape[2]
    mask = mask_ref[...] > 0
    for k in range(step_rows):
        row = jnp.concatenate([state_ref[k], cond_ref[k]], axis=0)
        d = jnp.dot(w1_ref[...], with_neighbours(row), preferred_element_type=jnp.float32)
        full = c1[...] + d[2 * out : 3 * out] + b1_ref[...]
        c1[...] = a1[...] + d[out : 2 * out]
        a1[...] = d[:out]
        y = step * step_rows + k - 3 + place[0]
        inside = mask & (y >= 0) & (y < place[1])
        hidden = jnp.where(inside, full / (1.0 + jnp.exp(-full)), 0.0).astype(BF)
        e = jnp.dot(w2_ref[...], with_neighbours(hidden), preferred_element_type=jnp.float32)
        o_ref[k] = (c2[...] + e[2 * out :] + b2_ref[...])[:, :width].astype(BF)
        c2[...] = a2[...] + e[out : 2 * out]
        a2[...] = e[:out] + d[3 * out :]


def denoise(state, cond, mask, place, first_kernel, first_bias, second_kernel, second_bias, shortcut, s_ch, width):
    tall, s_pad, lanes = state.shape
    c_pad = cond.shape[1]
    out, cin = shortcut.shape
    rows = tall - 4
    step_rows = 4

    def spread(w):
        zero = lambda n: jnp.zeros(w.shape[:-1] + (n,), w.dtype)
        return jnp.concatenate([w[..., :s_ch], zero(s_pad - s_ch), w[..., s_ch:], zero(c_pad - (cin - s_ch))], -1)

    w1 = spread(first_kernel).transpose(0, 2, 1, 3).reshape(3 * out, 3 * (s_pad + c_pad))
    skip = spread(shortcut)
    skip = jnp.concatenate([jnp.zeros_like(skip), skip, jnp.zeros_like(skip)], axis=1)
    w1 = jnp.concatenate([w1, skip], axis=0)
    w2 = second_kernel.transpose(0, 2, 1, 3).reshape(3 * out, 3 * out)
    whole = lambda shape: pl.BlockSpec(shape, lambda i: (0,) * len(shape))
    total = jax.ShapeDtypeStruct((rows, out, width), BF)
    scratch = pltpu.VMEM((out, lanes), jnp.float32)
    return pl.pallas_call(
        functools.partial(block_kernel, step_rows, out),
        out_shape=total,
        grid=(tall // step_rows,),
        in_specs=[
            pl.BlockSpec(memory_space=pltpu.SMEM),
            whole((1, lanes)),
            pl.BlockSpec((step_rows, s_pad, lanes), lambda i: (i, 0, 0)),
            pl.BlockSpec((step_rows, c_pad, lanes), lambda i: (i, 0, 0)),
            whole(w1.shape),
            whole((out, 1)),
            whole(w2.shape),
            whole((out, 1)),
        ],
        out_specs=pl.BlockSpec((step_rows, out, width), lambda i: (jnp.maximum(i - 1, 0), 0, 0)),
        scratch_shapes=[scratch] * 4,
        compiler_params=pltpu.CompilerParams(dimension_semantics=("arbitrary",)),
        cost_estimate=pl.CostEstimate(
            flops=2 * tall * lanes * (w1.size + w2.size),
            bytes_accessed=2 * (state.size + cond.size + total.size),
            transcendentals=tall * out * lanes,
        ),
    )(place, mask, state, cond, w1, first_bias[:, None], w2, second_bias[:, None])


def shards(
    global_field,
    regional_state,
    windows,
    longitude_weights,
    latitude_weights,
    first_kernel,
    first_bias,
    second_kernel,
    later_conv_bias,
    shortcut_weight,
):
    tiles = lax.axis_size("tile")
    regions = lax.axis_size("region")
    tile_index = lax.axis_index("tile")
    region_index = lax.axis_index("region")
    half = tiles // 2
    row_tiles = half // TCOLS
    rotation = tiles // 4 + 2
    position = (tile_index + rotation) % tiles
    domain_half = position // half
    within = position % half
    row_tile = within // TCOLS
    col_tile = within % TCOLS
    my_domain = 2 * region_index + domain_half
    state = regional_state[0]
    channels, rows, cols = state.shape
    field_channels = global_field.shape[0]

    pieces = windows_of_domains(
        global_field, windows, region_index, latitude_weights.shape[2], longitude_weights.shape[2]
    )
    share = pieces.shape[1]
    sent = pieces.reshape((regions, 2) + pieces.shape[1:])
    got = lax.all_to_all(sent, "region", split_axis=0, concat_axis=0, tiled=True)
    mine = got.astype(F32).sum(0).astype(BF)
    halves = [((t + rotation) % tiles) // half for t in range(tiles)]
    spread = jnp.stack([mine[h] for h in halves])
    window = lax.all_to_all(spread, "tile", split_axis=0, concat_axis=0, tiled=True)
    window = window.reshape((tiles * share,) + window.shape[2:])[:field_channels]

    own = lax.dynamic_index_in_dim(windows, my_domain, 0, keepdims=False)
    lon = lax.dynamic_index_in_dim(longitude_weights, my_domain, 0, keepdims=False)
    lon = lon * (jnp.arange(lon.shape[1]) < own[3]).astype(BF)[None, :]
    lon = lax.dynamic_slice_in_dim(jnp.pad(lon, ((2, 2), (0, 0))), col_tile * cols, cols + 4, 0)
    lat = lax.dynamic_index_in_dim(latitude_weights, domain_half, 0, keepdims=False)
    lat = lat * (jnp.arange(lat.shape[1]) < own[1]).astype(BF)[None, :]
    lat = lax.dynamic_slice_in_dim(jnp.pad(lat, ((2, 2), (0, 0))), row_tile * rows, rows + 4, 0)
    lat = jnp.roll(lat, own[0] % lat.shape[1], axis=1)

    lanes = 2 * cols
    lon = around(lon.T, lanes)
    bands = jnp.einsum("clk,kx->clx", window, lon, preferred_element_type=F32).astype(BF)
    condition = jnp.einsum("yl,clx->ycx", lat, bands, preferred_element_type=F32).astype(BF)
    condition = jnp.pad(condition, ((0, 0), (0, -field_channels % 16), (0, 0)))

    flat = state.transpose(1, 0, 2)
    left = passed_along(flat[:, :, cols - 2 :], "tile", 1) * (col_tile > 0).astype(BF)
    right = passed_along(flat[:, :, :2], "tile", -1) * (col_tile < TCOLS - 1).astype(BF)
    wide = around(jnp.concatenate([left, flat, right], axis=2), lanes)
    if row_tiles > 1:
        above = passed_along(wide[rows - 2 :], "tile", TCOLS) * (row_tile > 0).astype(BF)
        below = passed_along(wide[:2], "tile", -TCOLS) * (row_tile < row_tiles - 1).astype(BF)
        wide = jnp.concatenate([above, wide, below], axis=0)
        wide = jnp.pad(wide, ((0, 0), (0, -channels % 16), (0, 0)))
    else:
        wide = jnp.pad(wide, ((2, 2), (0, -channels % 16), (0, 0)))

    x = around(jnp.arange(-2, cols + 2) + col_tile * cols + 1, lanes) - 1
    mask = ((x >= 0) & (x < TCOLS * cols)).astype(F32)[None, :]
    place = jnp.stack([row_tile * rows, row_tiles * rows]).astype(jnp.int32)
    result = denoise(
        wide, condition, mask, place, first_kernel, first_bias, second_kernel, later_conv_bias, shortcut_weight,
        channels, cols,
    )
    return result.transpose(1, 0, 2)[None]


def solution(mesh):
    placed = (
        P(None, "tile", "region"),
        P(("region", "tile"), None, None, None),
        P(),
        P(),
        P("region", None, None),
        P(),
        P(),
        P(),
        P(),
        P(),
    )
    return jax.shard_map(
        shards,
        mesh=mesh,
        in_specs=placed,
        out_specs=P(("region", "tile"), None, None, None),
        check_vma=False,
    )
```

```python
import functools

import jax
import jax.numpy as jnp
from jax import lax
from jax.experimental import pallas as pl
from jax.experimental.pallas import tpu as pltpu
from jax.sharding import PartitionSpec as P

TCOLS = 4
BF = jnp.bfloat16
F32 = jnp.float32
MESH = pl.DeviceIdType.MESH


def passed_along(block, axis, distance):
    devices = range(lax.axis_size(axis))
    route = [((i - distance) % len(devices), i) for i in devices]
    return lax.ppermute(block, axis, route)


def windows_of_domains(field, windows, region_index, lat_window, lon_window):
    tiles = lax.axis_size("tile")
    channels, band, cols = field.shape
    share = -(-channels // tiles)
    starts = [owned_start(t, tiles, channels, share) for t in range(tiles)]
    split = jnp.stack([field[start : start + share] for start in starts])
    bands = lax.all_to_all(split, "tile", split_axis=0, concat_axis=0, tiled=True)
    per = lat_window // band
    groups = bands.reshape(tiles // per, per, share, band, cols)
    groups = groups.transpose(0, 2, 1, 3, 4).reshape(tiles // per, share, lat_window, cols)
    count = groups.shape[0]
    row = jnp.arange(lat_window)[None, :, None]
    col = jnp.arange(cols)[:, None] + region_index * cols
    pieces = []
    for domain in range(windows.shape[0]):
        group, shift = windows[domain, 0] // lat_window, windows[domain, 0] % lat_window
        here = lax.dynamic_index_in_dim(groups, group, 0, keepdims=False)
        following = lax.dynamic_index_in_dim(groups, jnp.minimum(group + 1, count - 1), 0, keepdims=False)
        rows = jnp.where(row >= shift, here, following)
        pick = (col == jnp.arange(lon_window)[None, :] + windows[domain, 2]).astype(BF)
        pieces.append(jnp.einsum("clj,jk->clk", rows, pick, preferred_element_type=F32).astype(BF))
    return jnp.stack(pieces)


def owned_start(peer, tiles, channels, share):
    return peer * (channels - share) // (tiles - 1)


def exchange_kernel(sizes, windows_ref, field_ref, pick_ref, o_ref, got1, send2, got2, send3, s1, r1, own1, s2, r2, s3, r3):
    tiles, regions, channels, share, chunk, lat_window, rotation = sizes
    me, region = lax.axis_index("tile"), lax.axis_index("region")
    chunks, half = share // chunk, tiles // 2
    domains = 2 * regions

    def tile_peer(p):
        return lax.rem(me + p, tiles)

    def region_peer(p):
        return lax.rem(region + p, regions)

    barrier = pltpu.get_barrier_semaphore()
    for p in range(1, tiles):
        pl.semaphore_signal(barrier, inc=1, device_id=(region, tile_peer(p)), device_id_type=MESH)
    for p in range(1, regions):
        pl.semaphore_signal(barrier, inc=1, device_id=(region_peer(p), me), device_id_type=MESH)
    pl.semaphore_wait(barrier, tiles + regions - 2)

    def first(k, p):
        peer = tile_peer(p)
        start = owned_start(peer, tiles, channels, share) + k * chunk
        return pltpu.make_async_remote_copy(
            src_ref=field_ref.at[pl.ds(start, chunk)], dst_ref=got1[k].at[me], send_sem=s1.at[k, peer],
            recv_sem=r1.at[k, me], device_id=(region, peer), device_id_type=MESH,
        )

    def first_from(k, p):
        peer = tile_peer(p)
        return pltpu.make_async_remote_copy(
            src_ref=got1[k].at[peer], dst_ref=got1[k].at[peer], send_sem=s1.at[k, peer],
            recv_sem=r1.at[k, peer], device_id=(region, peer), device_id_type=MESH,
        )

    def keep(k):
        start = owned_start(me, tiles, channels, share) + k * chunk
        return pltpu.make_async_copy(field_ref.at[pl.ds(start, chunk)], got1[k].at[me], own1.at[k])

    def second(k, p, source):
        peer = region_peer(p)
        return pltpu.make_async_remote_copy(
            src_ref=send2.at[k, peer], dst_ref=got2.at[k, peer if source else region], send_sem=s2.at[k, peer],
            recv_sem=r2.at[k, peer if source else region], device_id=(peer, me), device_id_type=MESH,
        )

    def third(k, p, source):
        peer = tile_peer(p)
        part = (lax.rem(peer + rotation, tiles)) // half
        return pltpu.make_async_remote_copy(
            src_ref=send3.at[k, part], dst_ref=o_ref.at[peer if source else me, pl.ds(k * chunk, chunk)],
            send_sem=s3.at[k, peer], recv_sem=r3.at[k, peer if source else me],
            device_id=(region, peer), device_id_type=MESH,
        )

    for k in range(chunks):
        keep(k).start()
        for p in range(1, tiles):
            first(k, p).start()

    def extract(k):
        for p in range(1, tiles):
            first_from(k, p).wait_recv()
        keep(k).wait()
        cols = pick_ref.shape[1]
        row = lax.broadcasted_iota(jnp.int32, (chunk, lat_window, cols), 1)
        for d in range(domains):
            group, shift = windows_ref[d, 0] // lat_window, lax.rem(windows_ref[d, 0], lat_window)
            here = got1[k][group]
            following = got1[k][jnp.minimum(group + 1, tiles - 1)]
            rows = jnp.where(row >= shift, here.astype(F32), following.astype(F32)).astype(BF)
            found = jnp.dot(rows.reshape(chunk * lat_window, cols), pick_ref[d], preferred_element_type=F32)
            send2[k, d // 2, d % 2] = found.astype(BF).reshape(chunk, lat_window, found.shape[1])
        got2[k, region] = send2[k, region]
        for p in range(1, regions):
            second(k, p, False).start()

    def combine(k):
        for p in range(1, regions):
            second(k, p, True).wait_recv()
        total = got2[k, 0]
        for r in range(1, regions):
            total = total + got2[k, r]
        send3[k] = total
        for p in range(1, tiles):
            third(k, p, False).start()
        o_ref[me, pl.ds(k * chunk, chunk)] = send3[k, lax.rem(me + rotation, tiles) // half]

    for k in range(chunks):
        extract(k)
        if k > 0:
            combine(k - 1)
    combine(chunks - 1)
    for k in range(chunks):
        for p in range(1, tiles):
            third(k, p, True).wait_recv()
    for k in range(chunks):
        for p in range(1, tiles):
            first(k, p).wait_send()
            third(k, p, False).wait_send()
        for p in range(1, regions):
            second(k, p, False).wait_send()


def exchange(field, windows, region_index, lat_window, lon_window, rotation):
    tiles, regions = lax.axis_size("tile"), lax.axis_size("region")
    channels, band, cols = field.shape
    share = -(-channels // tiles)
    chunk = max(n for n in (1, 2, 3) if share % n == 0)
    chunks = share // chunk
    col = jnp.arange(cols)[None, :, None] + region_index * cols
    pick = (col == jnp.arange(lon_window)[None, None, :] + windows[:, 2][:, None, None]).astype(BF)
    vmem = pl.BlockSpec(memory_space=pltpu.VMEM)
    block = (chunk, lat_window, lon_window)
    dma = pltpu.SemaphoreType.DMA
    return pl.pallas_call(
        functools.partial(exchange_kernel, (tiles, regions, channels, share, chunk, lat_window, rotation)),
        out_shape=jax.ShapeDtypeStruct((tiles, share, lat_window, lon_window), BF),
        in_specs=[pl.BlockSpec(memory_space=pltpu.SMEM), pl.BlockSpec(memory_space=pl.ANY), vmem],
        out_specs=vmem,
        scratch_shapes=[
            [pltpu.VMEM((tiles, chunk, band, cols), BF)] * chunks,
            pltpu.VMEM((chunks, regions, 2) + block, BF),
            pltpu.VMEM((chunks, regions, 2) + block, BF),
            pltpu.VMEM((chunks, 2) + block, BF),
            dma((chunks, tiles)),
            dma((chunks, tiles)),
            dma((chunks,)),
            dma((chunks, regions)),
            dma((chunks, regions)),
            dma((chunks, tiles)),
            dma((chunks, tiles)),
        ],
        compiler_params=pltpu.CompilerParams(collective_id=0, has_side_effects=True, vmem_limit_bytes=32 << 20),
    )(windows, field, pick)


def exchange_by_collectives(field, windows, region_index, lat_window, lon_window, rotation):
    tiles, regions = lax.axis_size("tile"), lax.axis_size("region")
    pieces = windows_of_domains(field, windows, region_index, lat_window, lon_window)
    sent = pieces.reshape((regions, 2) + pieces.shape[1:])
    got = lax.all_to_all(sent, "region", split_axis=0, concat_axis=0, tiled=True)
    mine = got.astype(F32).sum(0).astype(BF)
    halves = [((t + rotation) % tiles) // (tiles // 2) for t in range(tiles)]
    spread = jnp.stack([mine[h] for h in halves])
    return lax.all_to_all(spread, "tile", split_axis=0, concat_axis=0, tiled=True)


def around(value, lanes):
    zeros = jnp.zeros(value.shape[:-1] + (lanes - value.shape[-1],), value.dtype)
    return jnp.concatenate([value[..., 2:], zeros, value[..., :2]], axis=-1)


def with_neighbours(value):
    return jnp.concatenate([pltpu.roll(value, 1, 1), value, pltpu.roll(value, value.shape[1] - 1, 1)], axis=0)


def block_kernel(step_rows, out, place, mask_ref, state_ref, cond_ref, w1_ref, b1_ref, w2_ref, b2_ref, o_ref, a1, c1, a2, c2):
    step = pl.program_id(0)

    @pl.when(step == 0)
    def _():
        for ref in (a1, c1, a2, c2):
            ref[...] = jnp.zeros_like(ref)

    width = o_ref.shape[2]
    mask = mask_ref[...] > 0
    for k in range(step_rows):
        row = jnp.concatenate([state_ref[k], cond_ref[k]], axis=0)
        d = jnp.dot(w1_ref[...], with_neighbours(row), preferred_element_type=jnp.float32)
        full = c1[...] + d[2 * out : 3 * out] + b1_ref[...]
        c1[...] = a1[...] + d[out : 2 * out]
        a1[...] = d[:out]
        y = step * step_rows + k - 3 + place[0]
        inside = mask & (y >= 0) & (y < place[1])
        hidden = jnp.where(inside, full / (1.0 + jnp.exp(-full)), 0.0).astype(BF)
        e = jnp.dot(w2_ref[...], with_neighbours(hidden), preferred_element_type=jnp.float32)
        o_ref[k] = (c2[...] + e[2 * out :] + b2_ref[...])[:, :width].astype(BF)
        c2[...] = a2[...] + e[out : 2 * out]
        a2[...] = e[:out] + d[3 * out :]


def denoise(state, cond, mask, place, first_kernel, first_bias, second_kernel, second_bias, shortcut, s_ch, width, starts, share):
    tall, s_pad, lanes = state.shape
    c_pad = cond.shape[1]
    out, cin = shortcut.shape
    rows = tall - 4
    step_rows = 4

    def spread(w):
        zero = lambda n: jnp.zeros(w.shape[:-1] + (n,), w.dtype)
        parts = [w[..., :s_ch], zero(s_pad - s_ch)]
        done = s_ch
        for start in starts:
            seen = min(max(done - (s_ch + start), 0), share)
            end = s_ch + start + share
            parts += [zero(seen), w[..., end - share + seen : end]]
            done = max(done, end)
        return jnp.concatenate(parts + [zero(c_pad - share * len(starts))], -1)

    w1 = spread(first_kernel).transpose(0, 2, 1, 3).reshape(3 * out, 3 * (s_pad + c_pad))
    skip = spread(shortcut)
    skip = jnp.concatenate([jnp.zeros_like(skip), skip, jnp.zeros_like(skip)], axis=1)
    w1 = jnp.concatenate([w1, skip], axis=0)
    w2 = second_kernel.transpose(0, 2, 1, 3).reshape(3 * out, 3 * out)
    whole = lambda shape: pl.BlockSpec(shape, lambda i: (0,) * len(shape))
    total = jax.ShapeDtypeStruct((rows, out, width), BF)
    scratch = pltpu.VMEM((out, lanes), jnp.float32)
    return pl.pallas_call(
        functools.partial(block_kernel, step_rows, out),
        out_shape=total,
        grid=(tall // step_rows,),
        in_specs=[
            pl.BlockSpec(memory_space=pltpu.SMEM),
            whole((1, lanes)),
            pl.BlockSpec((step_rows, s_pad, lanes), lambda i: (i, 0, 0)),
            pl.BlockSpec((step_rows, c_pad, lanes), lambda i: (i, 0, 0)),
            whole(w1.shape),
            whole((out, 1)),
            whole(w2.shape),
            whole((out, 1)),
        ],
        out_specs=pl.BlockSpec((step_rows, out, width), lambda i: (jnp.maximum(i - 1, 0), 0, 0)),
        scratch_shapes=[scratch] * 4,
        compiler_params=pltpu.CompilerParams(dimension_semantics=("arbitrary",)),
        cost_estimate=pl.CostEstimate(
            flops=2 * tall * lanes * (w1.size + w2.size),
            bytes_accessed=2 * (state.size + cond.size + total.size),
            transcendentals=tall * out * lanes,
        ),
    )(place, mask, state, cond, w1, first_bias[:, None], w2, second_bias[:, None])


def shards(
    global_field,
    regional_state,
    windows,
    longitude_weights,
    latitude_weights,
    first_kernel,
    first_bias,
    second_kernel,
    later_conv_bias,
    shortcut_weight,
):
    tiles = lax.axis_size("tile")
    regions = lax.axis_size("region")
    tile_index = lax.axis_index("tile")
    region_index = lax.axis_index("region")
    half = tiles // 2
    row_tiles = half // TCOLS
    rotation = tiles // 4 + 2
    position = (tile_index + rotation) % tiles
    domain_half = position // half
    within = position % half
    row_tile = within // TCOLS
    col_tile = within % TCOLS
    my_domain = 2 * region_index + domain_half
    state = regional_state[0]
    channels, rows, cols = state.shape
    field_channels = global_field.shape[0]

    lat_window, lon_window = latitude_weights.shape[2], longitude_weights.shape[2]
    route = exchange if global_field.shape[1] == lat_window else exchange_by_collectives
    window = route(global_field, windows, region_index, lat_window, lon_window, rotation)
    share = window.shape[1]
    window = window.reshape((tiles * share,) + window.shape[2:])

    own = lax.dynamic_index_in_dim(windows, my_domain, 0, keepdims=False)
    lon = lax.dynamic_index_in_dim(longitude_weights, my_domain, 0, keepdims=False)
    lon = lon * (jnp.arange(lon.shape[1]) < own[3]).astype(BF)[None, :]
    lon = lax.dynamic_slice_in_dim(jnp.pad(lon, ((2, 2), (0, 0))), col_tile * cols, cols + 4, 0)
    lat = lax.dynamic_index_in_dim(latitude_weights, domain_half, 0, keepdims=False)
    lat = lat * (jnp.arange(lat.shape[1]) < own[1]).astype(BF)[None, :]
    lat = lax.dynamic_slice_in_dim(jnp.pad(lat, ((2, 2), (0, 0))), row_tile * rows, rows + 4, 0)
    lat = jnp.roll(lat, own[0] % lat.shape[1], axis=1)

    lanes = 2 * cols
    lon = around(lon.T, lanes)
    bands = jnp.einsum("clk,kx->clx", window, lon, preferred_element_type=F32).astype(BF)
    condition = jnp.einsum("yl,clx->ycx", lat, bands, preferred_element_type=F32).astype(BF)
    condition = jnp.pad(condition, ((0, 0), (0, -(tiles * share) % 16), (0, 0)))

    flat = state.transpose(1, 0, 2)
    left = passed_along(flat[:, :, cols - 2 :], "tile", 1) * (col_tile > 0).astype(BF)
    right = passed_along(flat[:, :, :2], "tile", -1) * (col_tile < TCOLS - 1).astype(BF)
    wide = around(jnp.concatenate([left, flat, right], axis=2), lanes)
    if row_tiles > 1:
        above = passed_along(wide[rows - 2 :], "tile", TCOLS) * (row_tile > 0).astype(BF)
        below = passed_along(wide[:2], "tile", -TCOLS) * (row_tile < row_tiles - 1).astype(BF)
        wide = jnp.concatenate([above, wide, below], axis=0)
        wide = jnp.pad(wide, ((0, 0), (0, -channels % 16), (0, 0)))
    else:
        wide = jnp.pad(wide, ((2, 2), (0, -channels % 16), (0, 0)))

    x = around(jnp.arange(-2, cols + 2) + col_tile * cols + 1, lanes) - 1
    mask = ((x >= 0) & (x < TCOLS * cols)).astype(F32)[None, :]
    place = jnp.stack([row_tile * rows, row_tiles * rows]).astype(jnp.int32)
    result = denoise(
        wide, condition, mask, place, first_kernel, first_bias, second_kernel, later_conv_bias, shortcut_weight,
        channels, cols, [owned_start(t, tiles, field_channels, share) for t in range(tiles)], share,
    )
    return result.transpose(1, 0, 2)[None]


def solution(mesh):
    placed = (
        P(None, "tile", "region"),
        P(("region", "tile"), None, None, None),
        P(),
        P(),
        P("region", None, None),
        P(),
        P(),
        P(),
        P(),
        P(),
    )
    return jax.shard_map(
        shards,
        mesh=mesh,
        in_specs=placed,
        out_specs=P(("region", "tile"), None, None, None),
        check_vma=False,
    )
```

```python
import functools

import jax
import jax.numpy as jnp
from jax import lax
from jax.experimental import pallas as pl
from jax.experimental.pallas import tpu as pltpu
from jax.sharding import PartitionSpec as P

TCOLS = 4
BF = jnp.bfloat16
F32 = jnp.float32
MESH = pl.DeviceIdType.MESH


def passed_along(block, axis, distance):
    devices = range(lax.axis_size(axis))
    route = [((i - distance) % len(devices), i) for i in devices]
    return lax.ppermute(block, axis, route)


def windows_of_domains(field, windows, region_index, lat_window, lon_window):
    tiles = lax.axis_size("tile")
    channels, band, cols = field.shape
    share = -(-channels // tiles)
    starts = [owned_start(t, tiles, channels, share) for t in range(tiles)]
    split = jnp.stack([field[start : start + share] for start in starts])
    bands = lax.all_to_all(split, "tile", split_axis=0, concat_axis=0, tiled=True)
    per = lat_window // band
    groups = bands.reshape(tiles // per, per, share, band, cols)
    groups = groups.transpose(0, 2, 1, 3, 4).reshape(tiles // per, share, lat_window, cols)
    count = groups.shape[0]
    row = jnp.arange(lat_window)[None, :, None]
    col = jnp.arange(cols)[:, None] + region_index * cols
    pieces = []
    for domain in range(windows.shape[0]):
        group, shift = windows[domain, 0] // lat_window, windows[domain, 0] % lat_window
        here = lax.dynamic_index_in_dim(groups, group, 0, keepdims=False)
        following = lax.dynamic_index_in_dim(groups, jnp.minimum(group + 1, count - 1), 0, keepdims=False)
        rows = jnp.where(row >= shift, here, following)
        pick = (col == jnp.arange(lon_window)[None, :] + windows[domain, 2]).astype(BF)
        pieces.append(jnp.einsum("clj,jk->clk", rows, pick, preferred_element_type=F32).astype(BF))
    return jnp.stack(pieces)


def owned_start(peer, tiles, channels, share):
    return peer * (channels - share) // (tiles - 1)


def exchange_kernel(
    sizes, windows_ref, field_ref, pick_ref, state_ref, w_ref, o_ref, part_ref, skip_ref,
    got1, send2, got2, send3, s1, r1, own1, s2, r2, s3, r3, edges, sides, padded, a1, c1, s4, r4,
):
    tiles, regions, channels, share, chunk, lat_window, rotation = sizes
    me, region = lax.axis_index("tile"), lax.axis_index("region")
    chunks, half = share // chunk, tiles // 2
    domains = 2 * regions

    def tile_peer(p):
        return lax.rem(me + p, tiles)

    def region_peer(p):
        return lax.rem(region + p, regions)

    rows, s_ch, width = state_ref.shape
    out = part_ref.shape[1]
    lane = lax.broadcasted_iota(jnp.int32, (s_ch, width), 1)
    column = lax.rem(lax.rem(me + rotation, tiles), TCOLS)

    def edge(side):
        peer = tile_peer(1 if side == 0 else tiles - 1)
        return pltpu.make_async_remote_copy(
            src_ref=edges.at[side], dst_ref=sides.at[side], send_sem=s4.at[side], recv_sem=r4.at[side],
            device_id=(region, peer), device_id_type=MESH,
        )

    barrier = pltpu.get_barrier_semaphore()
    for p in range(1, tiles):
        pl.semaphore_signal(barrier, inc=1, device_id=(region, tile_peer(p)), device_id_type=MESH)
    for p in range(1, regions):
        pl.semaphore_signal(barrier, inc=1, device_id=(region_peer(p), me), device_id_type=MESH)
    edges[...] = jnp.zeros_like(edges)

    def pack(y, packed):
        row = state_ref[y].astype(F32)
        last, first_two = packed
        here = (lane >= 2 * y) & (lane < 2 * y + 2)
        last = jnp.where(here, pltpu.roll(row, lax.rem(2 * y + 2, width), 1), last)
        first_two = jnp.where(here, pltpu.roll(row, 2 * y, 1), first_two)
        return last, first_two

    zero = jnp.zeros((s_ch, width), F32)
    last, first_two = lax.fori_loop(0, rows, pack, (zero, zero))
    edges[0, :s_ch] = last.astype(BF)
    edges[1, :s_ch] = first_two.astype(BF)
    padded[...] = jnp.zeros_like(padded)
    a1[...] = jnp.zeros_like(a1)
    c1[...] = jnp.zeros_like(c1)
    pl.semaphore_wait(barrier, tiles + regions - 2)
    for side in range(2):
        edge(side).start()

    def first(k, p):
        peer = tile_peer(p)
        start = owned_start(peer, tiles, channels, share) + k * chunk
        return pltpu.make_async_remote_copy(
            src_ref=field_ref.at[pl.ds(start, chunk)], dst_ref=got1[k].at[me], send_sem=s1.at[k, peer],
            recv_sem=r1.at[k, me], device_id=(region, peer), device_id_type=MESH,
        )

    def first_from(k, p):
        peer = tile_peer(p)
        return pltpu.make_async_remote_copy(
            src_ref=got1[k].at[peer], dst_ref=got1[k].at[peer], send_sem=s1.at[k, peer],
            recv_sem=r1.at[k, peer], device_id=(region, peer), device_id_type=MESH,
        )

    def keep(k):
        start = owned_start(me, tiles, channels, share) + k * chunk
        return pltpu.make_async_copy(field_ref.at[pl.ds(start, chunk)], got1[k].at[me], own1.at[k])

    def second(k, p, source):
        peer = region_peer(p)
        return pltpu.make_async_remote_copy(
            src_ref=send2.at[k, peer], dst_ref=got2.at[k, peer if source else region], send_sem=s2.at[k, peer],
            recv_sem=r2.at[k, peer if source else region], device_id=(peer, me), device_id_type=MESH,
        )

    def third(k, p, source):
        peer = tile_peer(p)
        part = (lax.rem(peer + rotation, tiles)) // half
        return pltpu.make_async_remote_copy(
            src_ref=send3.at[k, part], dst_ref=o_ref.at[pl.ds((peer if source else me) * share + k * chunk, chunk)],
            send_sem=s3.at[k, peer], recv_sem=r3.at[k, peer if source else me],
            device_id=(region, peer), device_id_type=MESH,
        )

    for k in range(chunks):
        keep(k).start()
        for p in range(1, tiles):
            first(k, p).start()

    def state_rows(begin, end):
        lane_f = lax.broadcasted_iota(jnp.int32, (padded.shape[0], width), 1)

        def one(y, _):
            padded[:s_ch] = state_ref[y]
            after = pltpu.roll(sides[1].astype(F32), lax.rem(width - 2 * y, width), 1)
            before = pltpu.roll(sides[0].astype(F32), lax.rem(2 * width - 2 - 2 * y, width), 1)
            halo = jnp.where((lane_f < 2) & (column < TCOLS - 1), after, 0.0)
            halo = jnp.where((lane_f >= width - 2) & (column > 0), before, halo)
            row = jnp.concatenate([padded[...], halo.astype(BF)], axis=1)
            d = jnp.dot(w_ref[...], with_neighbours(row), preferred_element_type=F32)
            part_ref[y + 2] = c1[...] + d[2 * out : 3 * out]
            c1[...] = a1[...] + d[out : 2 * out]
            a1[...] = d[:out]
            skip_ref[y + 2] = d[3 * out :, :width]
            return 0

        lax.fori_loop(begin, end, one, 0, unroll=2)

    def extract(k):
        for p in range(1, tiles):
            first_from(k, p).wait_recv()
        keep(k).wait()
        cols = pick_ref.shape[1]
        row = lax.broadcasted_iota(jnp.int32, (chunk, lat_window, cols), 1)
        for d in range(domains):
            group, shift = windows_ref[d, 0] // lat_window, lax.rem(windows_ref[d, 0], lat_window)
            here = got1[k][group]
            following = got1[k][jnp.minimum(group + 1, tiles - 1)]
            rows = jnp.where(row >= shift, here.astype(F32), following.astype(F32)).astype(BF)
            found = jnp.dot(rows.reshape(chunk * lat_window, cols), pick_ref[d], preferred_element_type=F32)
            send2[k, d // 2, d % 2] = found.astype(BF).reshape(chunk, lat_window, found.shape[1])
        got2[k, region] = send2[k, region]
        for p in range(1, regions):
            second(k, p, False).start()

    def combine(k):
        for p in range(1, regions):
            second(k, p, True).wait_recv()
        total = got2[k, 0]
        for r in range(1, regions):
            total = total + got2[k, r]
        send3[k] = total
        for p in range(1, tiles):
            third(k, p, False).start()
        o_ref[pl.ds(me * share + k * chunk, chunk)] = send3[k, lax.rem(me + rotation, tiles) // half]

    o_ref[tiles * share :] = jnp.zeros_like(o_ref[tiles * share :])
    for side in range(2):
        edge(side).wait_recv()
    cuts = [rows * n // (chunks + 1) // 2 * 2 for n in range(chunks + 1)] + [rows]
    for k in range(chunks):
        state_rows(cuts[k], cuts[k + 1])
        extract(k)
        if k > 0:
            combine(k - 1)
    state_rows(cuts[chunks], rows)
    part_ref[rows + 2] = c1[...]
    combine(chunks - 1)
    for k in range(chunks):
        for p in range(1, tiles):
            third(k, p, True).wait_recv()
    for side in range(2):
        edge(side).wait_send()
    for k in range(chunks):
        for p in range(1, tiles):
            first(k, p).wait_send()
            third(k, p, False).wait_send()
        for p in range(1, regions):
            second(k, p, False).wait_send()


def exchange(field, windows, state, weights, region_index, lat_window, lon_window, rotation):
    tiles, regions = lax.axis_size("tile"), lax.axis_size("region")
    channels, band, cols = field.shape
    share = -(-channels // tiles)
    chunk = max(n for n in (1, 2, 3) if share % n == 0)
    chunks = share // chunk
    rows, s_ch, width = state.shape
    out, s_pad = weights.shape[0] // 4, weights.shape[1] // 3
    held = tiles * share + -(tiles * share) % 16
    col = jnp.arange(cols)[None, :, None] + region_index * cols
    pick = (col == jnp.arange(lon_window)[None, None, :] + windows[:, 2][:, None, None]).astype(BF)
    vmem = pl.BlockSpec(memory_space=pltpu.VMEM)
    block = (chunk, lat_window, lon_window)
    dma = pltpu.SemaphoreType.DMA
    return pl.pallas_call(
        functools.partial(exchange_kernel, (tiles, regions, channels, share, chunk, lat_window, rotation)),
        out_shape=(
            jax.ShapeDtypeStruct((held, lat_window, lon_window), BF),
            jax.ShapeDtypeStruct((rows + 4, out, 2 * width), F32),
            jax.ShapeDtypeStruct((rows + 4, out, width), F32),
        ),
        in_specs=[pl.BlockSpec(memory_space=pltpu.SMEM), pl.BlockSpec(memory_space=pl.ANY), vmem, vmem, vmem],
        out_specs=(vmem, vmem, vmem),
        scratch_shapes=[
            [pltpu.VMEM((tiles, chunk, band, cols), BF)] * chunks,
            pltpu.VMEM((chunks, regions, 2) + block, BF),
            pltpu.VMEM((chunks, regions, 2) + block, BF),
            pltpu.VMEM((chunks, 2) + block, BF),
            dma((chunks, tiles)),
            dma((chunks, tiles)),
            dma((chunks,)),
            dma((chunks, regions)),
            dma((chunks, regions)),
            dma((chunks, tiles)),
            dma((chunks, tiles)),
            pltpu.VMEM((2, s_pad, width), BF),
            pltpu.VMEM((2, s_pad, width), BF),
            pltpu.VMEM((s_pad, width), BF),
            pltpu.VMEM((out, 2 * width), F32),
            pltpu.VMEM((out, 2 * width), F32),
            dma((2,)),
            dma((2,)),
        ],
        compiler_params=pltpu.CompilerParams(collective_id=0, has_side_effects=True, vmem_limit_bytes=40 << 20),
    )(windows, field, pick, state, weights)


def exchange_by_collectives(field, windows, region_index, lat_window, lon_window, rotation):
    tiles, regions = lax.axis_size("tile"), lax.axis_size("region")
    pieces = windows_of_domains(field, windows, region_index, lat_window, lon_window)
    sent = pieces.reshape((regions, 2) + pieces.shape[1:])
    got = lax.all_to_all(sent, "region", split_axis=0, concat_axis=0, tiled=True)
    mine = got.astype(F32).sum(0).astype(BF)
    halves = [((t + rotation) % tiles) // (tiles // 2) for t in range(tiles)]
    spread = jnp.stack([mine[h] for h in halves])
    return lax.all_to_all(spread, "tile", split_axis=0, concat_axis=0, tiled=True)


def around(value, lanes):
    zeros = jnp.zeros(value.shape[:-1] + (lanes - value.shape[-1],), value.dtype)
    return jnp.concatenate([value[..., 2:], zeros, value[..., :2]], axis=-1)


def with_neighbours(value):
    return jnp.concatenate([pltpu.roll(value, 1, 1), value, pltpu.roll(value, value.shape[1] - 1, 1)], axis=0)


def block_kernel(step_rows, out, place, mask_ref, state_ref, cond_ref, w1_ref, b1_ref, w2_ref, b2_ref, o_ref, a1, c1, a2, c2):
    step = pl.program_id(0)

    @pl.when(step == 0)
    def _():
        for ref in (a1, c1, a2, c2):
            ref[...] = jnp.zeros_like(ref)

    width = o_ref.shape[2]
    mask = mask_ref[...] > 0
    for k in range(step_rows):
        row = jnp.concatenate([state_ref[k], cond_ref[k]], axis=0)
        d = jnp.dot(w1_ref[...], with_neighbours(row), preferred_element_type=jnp.float32)
        full = c1[...] + d[2 * out : 3 * out] + b1_ref[...]
        c1[...] = a1[...] + d[out : 2 * out]
        a1[...] = d[:out]
        y = step * step_rows + k - 3 + place[0]
        inside = mask & (y >= 0) & (y < place[1])
        hidden = jnp.where(inside, full / (1.0 + jnp.exp(-full)), 0.0).astype(BF)
        e = jnp.dot(w2_ref[...], with_neighbours(hidden), preferred_element_type=jnp.float32)
        o_ref[k] = (c2[...] + e[2 * out :] + b2_ref[...])[:, :width].astype(BF)
        c2[...] = a2[...] + e[out : 2 * out]
        a2[...] = e[:out] + d[3 * out :]


def finish_kernel(step_rows, rows, out, mask_ref, cond_ref, part_ref, skip_ref, w1_ref, b1_ref, w2_ref, b2_ref, o_ref, a1, c1, a2, c2):
    step = pl.program_id(0)

    @pl.when(step == 0)
    def _():
        for ref in (a1, c1, a2, c2):
            ref[...] = jnp.zeros_like(ref)

    width = o_ref.shape[2]
    mask = mask_ref[...] > 0
    for k in range(step_rows):
        d = jnp.dot(w1_ref[...], with_neighbours(cond_ref[k]), preferred_element_type=jnp.float32)
        full = c1[...] + d[2 * out : 3 * out] + (part_ref[k] + b1_ref[...])
        c1[...] = a1[...] + d[out : 2 * out]
        a1[...] = d[:out]
        y = step * step_rows + k - 3
        inside = mask & (y >= 0) & (y < rows)
        hidden = jnp.where(inside, full / (1.0 + jnp.exp(-full)), 0.0).astype(BF)
        near = with_neighbours(hidden)[:, :width]
        e = jnp.dot(w2_ref[...], near, preferred_element_type=jnp.float32)
        o_ref[k] = (c2[...] + e[2 * out :] + b2_ref[...]).astype(BF)
        c2[...] = a2[...] + e[out : 2 * out]
        a2[...] = e[:out] + (d[3 * out :, :width] + skip_ref[k])


def laid_out(kernel, shortcut):
    out, cin = shortcut.shape
    w = kernel.transpose(0, 2, 1, 3).reshape(3 * out, 3 * cin)
    skip = jnp.concatenate([jnp.zeros_like(shortcut), shortcut, jnp.zeros_like(shortcut)], axis=1)
    return jnp.concatenate([w, skip], axis=0)


def padded_to(w, size):
    return jnp.concatenate([w, jnp.zeros(w.shape[:-1] + (size - w.shape[-1],), w.dtype)], -1)


def of_groups(w, starts, share, size):
    parts, done = [], 0
    for start in starts:
        seen = min(max(done - start, 0), share)
        parts += [jnp.zeros(w.shape[:-1] + (seen,), w.dtype), w[..., start + seen : start + share]]
        done = max(done, start + share)
    return padded_to(jnp.concatenate(parts, -1), size)


def finish(cond, part, skip, mask, w1, first_bias, w2, second_bias, width):
    tall, c_pad, lanes = cond.shape
    out = part.shape[1]
    rows, step_rows = tall - 4, 4
    whole = lambda shape: pl.BlockSpec(shape, lambda i: (0,) * len(shape))
    by_row = lambda x: pl.BlockSpec((step_rows,) + x.shape[1:], lambda i: (i, 0, 0))
    total = jax.ShapeDtypeStruct((rows, out, width), BF)
    return pl.pallas_call(
        functools.partial(finish_kernel, step_rows, rows, out),
        out_shape=total,
        grid=(tall // step_rows,),
        in_specs=[whole((1, lanes)), by_row(cond), by_row(part), by_row(skip), whole(w1.shape), whole((out, 1)),
                  whole(w2.shape), whole((out, 1))],
        out_specs=pl.BlockSpec((step_rows, out, width), lambda i: (jnp.maximum(i - 1, 0), 0, 0)),
        scratch_shapes=[pltpu.VMEM((out, lanes), F32)] * 2 + [pltpu.VMEM((out, width), F32)] * 2,
        compiler_params=pltpu.CompilerParams(dimension_semantics=("arbitrary",), vmem_limit_bytes=32 << 20),
    )(mask, cond, part, skip, w1, first_bias[:, None], w2, second_bias[:, None])


def denoise(state, cond, mask, place, first_kernel, first_bias, second_kernel, second_bias, shortcut, s_ch, width, starts, share):
    tall, s_pad, lanes = state.shape
    c_pad = cond.shape[1]
    out, cin = shortcut.shape
    rows = tall - 4
    step_rows = 4

    def spread(w):
        zero = lambda n: jnp.zeros(w.shape[:-1] + (n,), w.dtype)
        parts = [w[..., :s_ch], zero(s_pad - s_ch)]
        done = s_ch
        for start in starts:
            seen = min(max(done - (s_ch + start), 0), share)
            end = s_ch + start + share
            parts += [zero(seen), w[..., end - share + seen : end]]
            done = max(done, end)
        return jnp.concatenate(parts + [zero(c_pad - share * len(starts))], -1)

    w1 = spread(first_kernel).transpose(0, 2, 1, 3).reshape(3 * out, 3 * (s_pad + c_pad))
    skip = spread(shortcut)
    skip = jnp.concatenate([jnp.zeros_like(skip), skip, jnp.zeros_like(skip)], axis=1)
    w1 = jnp.concatenate([w1, skip], axis=0)
    w2 = second_kernel.transpose(0, 2, 1, 3).reshape(3 * out, 3 * out)
    whole = lambda shape: pl.BlockSpec(shape, lambda i: (0,) * len(shape))
    total = jax.ShapeDtypeStruct((rows, out, width), BF)
    scratch = pltpu.VMEM((out, lanes), jnp.float32)
    return pl.pallas_call(
        functools.partial(block_kernel, step_rows, out),
        out_shape=total,
        grid=(tall // step_rows,),
        in_specs=[
            pl.BlockSpec(memory_space=pltpu.SMEM),
            whole((1, lanes)),
            pl.BlockSpec((step_rows, s_pad, lanes), lambda i: (i, 0, 0)),
            pl.BlockSpec((step_rows, c_pad, lanes), lambda i: (i, 0, 0)),
            whole(w1.shape),
            whole((out, 1)),
            whole(w2.shape),
            whole((out, 1)),
        ],
        out_specs=pl.BlockSpec((step_rows, out, width), lambda i: (jnp.maximum(i - 1, 0), 0, 0)),
        scratch_shapes=[scratch] * 4,
        compiler_params=pltpu.CompilerParams(dimension_semantics=("arbitrary",)),
        cost_estimate=pl.CostEstimate(
            flops=2 * tall * lanes * (w1.size + w2.size),
            bytes_accessed=2 * (state.size + cond.size + total.size),
            transcendentals=tall * out * lanes,
        ),
    )(place, mask, state, cond, w1, first_bias[:, None], w2, second_bias[:, None])


def shards(
    global_field,
    regional_state,
    windows,
    longitude_weights,
    latitude_weights,
    first_kernel,
    first_bias,
    second_kernel,
    later_conv_bias,
    shortcut_weight,
):
    tiles = lax.axis_size("tile")
    regions = lax.axis_size("region")
    tile_index = lax.axis_index("tile")
    region_index = lax.axis_index("region")
    half = tiles // 2
    row_tiles = half // TCOLS
    rotation = tiles // 4 + 2
    position = (tile_index + rotation) % tiles
    domain_half = position // half
    within = position % half
    row_tile = within // TCOLS
    col_tile = within % TCOLS
    my_domain = 2 * region_index + domain_half
    state = regional_state[0]
    channels, rows, cols = state.shape
    field_channels = global_field.shape[0]

    lat_window, lon_window = latitude_weights.shape[2], longitude_weights.shape[2]
    share = -(-field_channels // tiles)
    starts = [owned_start(t, tiles, field_channels, share) for t in range(tiles)]
    out = shortcut_weight.shape[0]
    flat = state.transpose(1, 0, 2)
    fused = global_field.shape[1] == lat_window and row_tiles == 1
    if fused:
        s_pad, c_pad = channels + -channels % 16, tiles * share + -(tiles * share) % 16
        w_state = laid_out(padded_to(first_kernel[..., :channels], s_pad), padded_to(shortcut_weight[:, :channels], s_pad))
        w_cond = laid_out(
            of_groups(first_kernel[..., channels:], starts, share, c_pad),
            of_groups(shortcut_weight[:, channels:], starts, share, c_pad),
        )
        window, part, skip = exchange(
            global_field, windows, flat, w_state, region_index, lat_window, lon_window, rotation
        )
    else:
        window = exchange_by_collectives(global_field, windows, region_index, lat_window, lon_window, rotation)
        window = window.reshape((tiles * share,) + window.shape[2:])

    own = lax.dynamic_index_in_dim(windows, my_domain, 0, keepdims=False)
    lon = lax.dynamic_index_in_dim(longitude_weights, my_domain, 0, keepdims=False)
    lon = lon * (jnp.arange(lon.shape[1]) < own[3]).astype(BF)[None, :]
    lon = lax.dynamic_slice_in_dim(jnp.pad(lon, ((2, 2), (0, 0))), col_tile * cols, cols + 4, 0)
    lat = lax.dynamic_index_in_dim(latitude_weights, domain_half, 0, keepdims=False)
    lat = lat * (jnp.arange(lat.shape[1]) < own[1]).astype(BF)[None, :]
    lat = lax.dynamic_slice_in_dim(jnp.pad(lat, ((2, 2), (0, 0))), row_tile * rows, rows + 4, 0)
    lat = jnp.roll(lat, own[0] % lat.shape[1], axis=1)

    lanes = 2 * cols
    lon = around(lon.T, lanes)
    bands = jnp.einsum("clk,kx->clx", window, lon, preferred_element_type=F32).astype(BF)
    condition = jnp.einsum("yl,clx->ycx", lat, bands, preferred_element_type=F32).astype(BF)
    condition = jnp.pad(condition, ((0, 0), (0, -condition.shape[1] % 16), (0, 0)))

    x = around(jnp.arange(-2, cols + 2) + col_tile * cols + 1, lanes) - 1
    mask = ((x >= 0) & (x < TCOLS * cols)).astype(F32)[None, :]
    if fused:
        w2 = second_kernel.transpose(0, 2, 1, 3).reshape(3 * out, 3 * out)
        result = finish(condition, part, skip, mask, w_cond, first_bias, w2, later_conv_bias, cols)
        return result.transpose(1, 0, 2)[None]

    left = passed_along(flat[:, :, cols - 2 :], "tile", 1) * (col_tile > 0).astype(BF)
    right = passed_along(flat[:, :, :2], "tile", -1) * (col_tile < TCOLS - 1).astype(BF)
    wide = around(jnp.concatenate([left, flat, right], axis=2), lanes)
    if row_tiles > 1:
        above = passed_along(wide[rows - 2 :], "tile", TCOLS) * (row_tile > 0).astype(BF)
        below = passed_along(wide[:2], "tile", -TCOLS) * (row_tile < row_tiles - 1).astype(BF)
        wide = jnp.concatenate([above, wide, below], axis=0)
        wide = jnp.pad(wide, ((0, 0), (0, -channels % 16), (0, 0)))
    else:
        wide = jnp.pad(wide, ((2, 2), (0, -channels % 16), (0, 0)))

    place = jnp.stack([row_tile * rows, row_tiles * rows]).astype(jnp.int32)
    result = denoise(
        wide, condition, mask, place, first_kernel, first_bias, second_kernel, later_conv_bias, shortcut_weight,
        channels, cols, starts, share,
    )
    return result.transpose(1, 0, 2)[None]


def solution(mesh):
    placed = (
        P(None, "tile", "region"),
        P(("region", "tile"), None, None, None),
        P(),
        P(),
        P("region", None, None),
        P(),
        P(),
        P(),
        P(),
        P(),
    )
    return jax.shard_map(
        shards,
        mesh=mesh,
        in_specs=placed,
        out_specs=P(("region", "tile"), None, None, None),
        check_vma=False,
    )
```

```python
import functools

import jax
import jax.numpy as jnp
from jax import lax
from jax.experimental import pallas as pl
from jax.experimental.pallas import tpu as pltpu
from jax.sharding import PartitionSpec as P

TCOLS = 4
BF = jnp.bfloat16
F32 = jnp.float32
MESH = pl.DeviceIdType.MESH


def passed_along(block, axis, distance):
    devices = range(lax.axis_size(axis))
    route = [((i - distance) % len(devices), i) for i in devices]
    return lax.ppermute(block, axis, route)


def windows_of_domains(field, windows, region_index, lat_window, lon_window):
    tiles = lax.axis_size("tile")
    channels, band, cols = field.shape
    share = -(-channels // tiles)
    starts = [owned_start(t, tiles, channels, share) for t in range(tiles)]
    split = jnp.stack([field[start : start + share] for start in starts])
    bands = lax.all_to_all(split, "tile", split_axis=0, concat_axis=0, tiled=True)
    per = lat_window // band
    groups = bands.reshape(tiles // per, per, share, band, cols)
    groups = groups.transpose(0, 2, 1, 3, 4).reshape(tiles // per, share, lat_window, cols)
    count = groups.shape[0]
    row = jnp.arange(lat_window)[None, :, None]
    col = jnp.arange(cols)[:, None] + region_index * cols
    pieces = []
    for domain in range(windows.shape[0]):
        group, shift = windows[domain, 0] // lat_window, windows[domain, 0] % lat_window
        here = lax.dynamic_index_in_dim(groups, group, 0, keepdims=False)
        following = lax.dynamic_index_in_dim(groups, jnp.minimum(group + 1, count - 1), 0, keepdims=False)
        rows = jnp.where(row >= shift, here, following)
        pick = (col == jnp.arange(lon_window)[None, :] + windows[domain, 2]).astype(BF)
        pieces.append(jnp.einsum("clj,jk->clk", rows, pick, preferred_element_type=F32).astype(BF))
    return jnp.stack(pieces)


def owned_start(peer, tiles, channels, share):
    return peer * (channels - share) // (tiles - 1)


def exchange_kernel(
    sizes, windows_ref, field_ref, pick_ref, state_ref, w_ref, o_ref, part_out, skip_out,
    got1, send2, got2, send3, s1, r1, own1, s2, r2, s3, r3, edges, sides, padded, a1, c1, s4, r4, part_ref, skip_ref, leave1, leave2,
):
    tiles, regions, channels, share, chunk, lat_window, rotation = sizes
    me, region = lax.axis_index("tile"), lax.axis_index("region")
    chunks, half = share // chunk, tiles // 2
    domains = 2 * regions

    def tile_peer(p):
        return lax.rem(me + p, tiles)

    def region_peer(p):
        return lax.rem(region + p, regions)

    rows, s_ch, width = state_ref.shape
    out = part_ref.shape[1]
    lane = lax.broadcasted_iota(jnp.int32, (s_ch, width), 1)
    column = lax.rem(lax.rem(me + rotation, tiles), TCOLS)

    def edge(side):
        peer = tile_peer(1 if side == 0 else tiles - 1)
        return pltpu.make_async_remote_copy(
            src_ref=edges.at[side], dst_ref=sides.at[side], send_sem=s4.at[side], recv_sem=r4.at[side],
            device_id=(region, peer), device_id_type=MESH,
        )

    barrier = pltpu.get_barrier_semaphore()
    for p in range(1, tiles):
        pl.semaphore_signal(barrier, inc=1, device_id=(region, tile_peer(p)), device_id_type=MESH)
    for p in range(1, regions):
        pl.semaphore_signal(barrier, inc=1, device_id=(region_peer(p), me), device_id_type=MESH)
    edges[...] = jnp.zeros_like(edges)

    def pack(y, packed):
        row = state_ref[y].astype(F32)
        last, first_two = packed
        here = (lane >= 2 * y) & (lane < 2 * y + 2)
        last = jnp.where(here, pltpu.roll(row, lax.rem(2 * y + 2, width), 1), last)
        first_two = jnp.where(here, pltpu.roll(row, 2 * y, 1), first_two)
        return last, first_two

    zero = jnp.zeros((s_ch, width), F32)
    last, first_two = lax.fori_loop(0, rows, pack, (zero, zero))
    edges[0, :s_ch] = last.astype(BF)
    edges[1, :s_ch] = first_two.astype(BF)
    padded[...] = jnp.zeros_like(padded)
    a1[...] = jnp.zeros_like(a1)
    c1[...] = jnp.zeros_like(c1)
    pl.semaphore_wait(barrier, tiles + regions - 2)
    for side in range(2):
        edge(side).start()

    def first(k, p):
        peer = tile_peer(p)
        start = owned_start(peer, tiles, channels, share) + k * chunk
        return pltpu.make_async_remote_copy(
            src_ref=field_ref.at[pl.ds(start, chunk)], dst_ref=got1[k].at[me], send_sem=s1.at[k, peer],
            recv_sem=r1.at[k, me], device_id=(region, peer), device_id_type=MESH,
        )

    def first_from(k, p):
        peer = tile_peer(p)
        return pltpu.make_async_remote_copy(
            src_ref=got1[k].at[peer], dst_ref=got1[k].at[peer], send_sem=s1.at[k, peer],
            recv_sem=r1.at[k, peer], device_id=(region, peer), device_id_type=MESH,
        )

    def keep(k):
        start = owned_start(me, tiles, channels, share) + k * chunk
        return pltpu.make_async_copy(field_ref.at[pl.ds(start, chunk)], got1[k].at[me], own1.at[k])

    def second(k, p, source):
        peer = region_peer(p)
        return pltpu.make_async_remote_copy(
            src_ref=send2.at[k, peer], dst_ref=got2.at[k, peer if source else region], send_sem=s2.at[k, peer],
            recv_sem=r2.at[k, peer if source else region], device_id=(peer, me), device_id_type=MESH,
        )

    def third(k, p, source):
        peer = tile_peer(p)
        part = (lax.rem(peer + rotation, tiles)) // half
        return pltpu.make_async_remote_copy(
            src_ref=send3.at[k, part], dst_ref=o_ref.at[pl.ds((peer if source else me) * share + k * chunk, chunk)],
            send_sem=s3.at[k, peer], recv_sem=r3.at[k, peer if source else me],
            device_id=(region, peer), device_id_type=MESH,
        )

    for k in range(chunks):
        keep(k).start()
        for p in range(1, tiles):
            first(k, p).start()

    cuts = [rows * n // (chunks + 1) // 2 * 2 for n in range(chunks + 1)] + [rows]

    def state_rows(begin, end):
        lane_f = lax.broadcasted_iota(jnp.int32, (padded.shape[0], width), 1)

        def one(y, _):
            padded[:s_ch] = state_ref[y]
            after = pltpu.roll(sides[1].astype(F32), lax.rem(width - 2 * y, width), 1)
            before = pltpu.roll(sides[0].astype(F32), lax.rem(2 * width - 2 - 2 * y, width), 1)
            halo = jnp.where((lane_f < 2) & (column < TCOLS - 1), after, 0.0)
            halo = jnp.where((lane_f >= width - 2) & (column > 0), before, halo)
            row = jnp.concatenate([padded[...], halo.astype(BF)], axis=1)
            d = jnp.dot(w_ref[...], with_neighbours(row), preferred_element_type=F32)
            part_ref[y + 2] = c1[...] + d[2 * out : 3 * out]
            c1[...] = a1[...] + d[out : 2 * out]
            a1[...] = d[:out]
            skip_ref[y + 2] = d[3 * out :, :width]
            return 0

        lax.fori_loop(begin, end, one, 0, unroll=2)

    def leave(n):
        begin, end = cuts[n] + 2, cuts[n + 1] + (3 if n == chunks else 2)
        span = pl.ds(begin, end - begin)
        return (
            pltpu.make_async_copy(part_ref.at[span], part_out.at[span], leave1.at[n]),
            pltpu.make_async_copy(skip_ref.at[span], skip_out.at[span], leave2.at[n]),
        )

    def extract(k):
        for p in range(1, tiles):
            first_from(k, p).wait_recv()
        keep(k).wait()
        cols = pick_ref.shape[1]
        row = lax.broadcasted_iota(jnp.int32, (chunk, lat_window, cols), 1)
        for d in range(domains):
            group, shift = windows_ref[d, 0] // lat_window, lax.rem(windows_ref[d, 0], lat_window)
            here = got1[k][group]
            following = got1[k][jnp.minimum(group + 1, tiles - 1)]
            rows = jnp.where(row >= shift, here.astype(F32), following.astype(F32)).astype(BF)
            found = jnp.dot(rows.reshape(chunk * lat_window, cols), pick_ref[d], preferred_element_type=F32)
            send2[k, d // 2, d % 2] = found.astype(BF).reshape(chunk, lat_window, found.shape[1])
        got2[k, region] = send2[k, region]
        for p in range(1, regions):
            second(k, p, False).start()

    def combine(k):
        for p in range(1, regions):
            second(k, p, True).wait_recv()
        total = got2[k, 0]
        for r in range(1, regions):
            total = total + got2[k, r]
        send3[k] = total
        for p in range(1, tiles):
            third(k, p, False).start()
        o_ref[pl.ds(me * share + k * chunk, chunk)] = send3[k, lax.rem(me + rotation, tiles) // half]

    o_ref[tiles * share :] = jnp.zeros_like(o_ref[tiles * share :])
    for side in range(2):
        edge(side).wait_recv()
    for k in range(chunks):
        state_rows(cuts[k], cuts[k + 1])
        for copy in leave(k):
            copy.start()
        extract(k)
        if k > 0:
            combine(k - 1)
    state_rows(cuts[chunks], rows)
    part_ref[rows + 2] = c1[...]
    skip_ref[rows + 2] = jnp.zeros(skip_ref.shape[1:], F32)
    for copy in leave(chunks):
        copy.start()
    combine(chunks - 1)
    for k in range(chunks):
        for p in range(1, tiles):
            third(k, p, True).wait_recv()
    for n in range(chunks + 1):
        for copy in leave(n):
            copy.wait()
    for side in range(2):
        edge(side).wait_send()
    for k in range(chunks):
        for p in range(1, tiles):
            first(k, p).wait_send()
            third(k, p, False).wait_send()
        for p in range(1, regions):
            second(k, p, False).wait_send()


def exchange(field, windows, state, weights, region_index, lat_window, lon_window, rotation):
    tiles, regions = lax.axis_size("tile"), lax.axis_size("region")
    channels, band, cols = field.shape
    share = -(-channels // tiles)
    chunk = max(n for n in (1, 2, 3) if share % n == 0)
    chunks = share // chunk
    rows, s_ch, width = state.shape
    out, s_pad = weights.shape[0] // 4, weights.shape[1] // 3
    held = tiles * share + -(tiles * share) % 16
    col = jnp.arange(cols)[None, :, None] + region_index * cols
    pick = (col == jnp.arange(lon_window)[None, None, :] + windows[:, 2][:, None, None]).astype(BF)
    vmem = pl.BlockSpec(memory_space=pltpu.VMEM)
    block = (chunk, lat_window, lon_window)
    dma = pltpu.SemaphoreType.DMA
    return pl.pallas_call(
        functools.partial(exchange_kernel, (tiles, regions, channels, share, chunk, lat_window, rotation)),
        out_shape=(
            jax.ShapeDtypeStruct((held, lat_window, lon_window), BF),
            jax.ShapeDtypeStruct((rows + 4, out, 2 * width), F32),
            jax.ShapeDtypeStruct((rows + 4, out, width), F32),
        ),
        in_specs=[pl.BlockSpec(memory_space=pltpu.SMEM), pl.BlockSpec(memory_space=pl.ANY), vmem, vmem, vmem],
        out_specs=(vmem, pl.BlockSpec(memory_space=pl.ANY), pl.BlockSpec(memory_space=pl.ANY)),
        scratch_shapes=[
            [pltpu.VMEM((tiles, chunk, band, cols), BF)] * chunks,
            pltpu.VMEM((chunks, regions, 2) + block, BF),
            pltpu.VMEM((chunks, regions, 2) + block, BF),
            pltpu.VMEM((chunks, 2) + block, BF),
            dma((chunks, tiles)),
            dma((chunks, tiles)),
            dma((chunks,)),
            dma((chunks, regions)),
            dma((chunks, regions)),
            dma((chunks, tiles)),
            dma((chunks, tiles)),
            pltpu.VMEM((2, s_pad, width), BF),
            pltpu.VMEM((2, s_pad, width), BF),
            pltpu.VMEM((s_pad, width), BF),
            pltpu.VMEM((out, 2 * width), F32),
            pltpu.VMEM((out, 2 * width), F32),
            dma((2,)),
            dma((2,)),
            pltpu.VMEM((rows + 4, out, 2 * width), F32),
            pltpu.VMEM((rows + 4, out, width), F32),
            dma((chunks + 1,)),
            dma((chunks + 1,)),
        ],
        compiler_params=pltpu.CompilerParams(collective_id=0, has_side_effects=True, vmem_limit_bytes=60 << 20),
    )(windows, field, pick, state, weights)


def exchange_by_collectives(field, windows, region_index, lat_window, lon_window, rotation):
    tiles, regions = lax.axis_size("tile"), lax.axis_size("region")
    pieces = windows_of_domains(field, windows, region_index, lat_window, lon_window)
    sent = pieces.reshape((regions, 2) + pieces.shape[1:])
    got = lax.all_to_all(sent, "region", split_axis=0, concat_axis=0, tiled=True)
    mine = got.astype(F32).sum(0).astype(BF)
    halves = [((t + rotation) % tiles) // (tiles // 2) for t in range(tiles)]
    spread = jnp.stack([mine[h] for h in halves])
    return lax.all_to_all(spread, "tile", split_axis=0, concat_axis=0, tiled=True)


def around(value, lanes):
    zeros = jnp.zeros(value.shape[:-1] + (lanes - value.shape[-1],), value.dtype)
    return jnp.concatenate([value[..., 2:], zeros, value[..., :2]], axis=-1)


def with_neighbours(value):
    return jnp.concatenate([pltpu.roll(value, 1, 1), value, pltpu.roll(value, value.shape[1] - 1, 1)], axis=0)


def block_kernel(step_rows, out, place, mask_ref, state_ref, cond_ref, w1_ref, b1_ref, w2_ref, b2_ref, o_ref, a1, c1, a2, c2):
    step = pl.program_id(0)

    @pl.when(step == 0)
    def _():
        for ref in (a1, c1, a2, c2):
            ref[...] = jnp.zeros_like(ref)

    width = o_ref.shape[2]
    mask = mask_ref[...] > 0
    for k in range(step_rows):
        row = jnp.concatenate([state_ref[k], cond_ref[k]], axis=0)
        d = jnp.dot(w1_ref[...], with_neighbours(row), preferred_element_type=jnp.float32)
        full = c1[...] + d[2 * out : 3 * out] + b1_ref[...]
        c1[...] = a1[...] + d[out : 2 * out]
        a1[...] = d[:out]
        y = step * step_rows + k - 3 + place[0]
        inside = mask & (y >= 0) & (y < place[1])
        hidden = jnp.where(inside, full / (1.0 + jnp.exp(-full)), 0.0).astype(BF)
        e = jnp.dot(w2_ref[...], with_neighbours(hidden), preferred_element_type=jnp.float32)
        o_ref[k] = (c2[...] + e[2 * out :] + b2_ref[...])[:, :width].astype(BF)
        c2[...] = a2[...] + e[out : 2 * out]
        a2[...] = e[:out] + d[3 * out :]


def finish_kernel(step_rows, rows, out, mask_ref, lon_ref, cond_ref, part_ref, skip_ref, w1_ref, b1_ref, w2_ref, b2_ref, o_ref, a1, c1, a2, c2):
    step = pl.program_id(0)

    @pl.when(step == 0)
    def _():
        for ref in (a1, c1, a2, c2):
            ref[...] = jnp.zeros_like(ref)

    width = o_ref.shape[2]
    mask = mask_ref[...] > 0
    c_pad, depth = cond_ref.shape[1:]
    cond = jnp.dot(cond_ref[...].reshape(step_rows * c_pad, depth), lon_ref[...], preferred_element_type=F32).astype(BF)
    for k in range(step_rows):
        d = jnp.dot(w1_ref[...], with_neighbours(cond[k * c_pad : (k + 1) * c_pad]), preferred_element_type=jnp.float32)
        full = c1[...] + d[2 * out : 3 * out] + (part_ref[k] + b1_ref[...])
        c1[...] = a1[...] + d[out : 2 * out]
        a1[...] = d[:out]
        y = step * step_rows + k - 3
        inside = mask & (y >= 0) & (y < rows)
        hidden = jnp.where(inside, full / (1.0 + jnp.exp(-full)), 0.0).astype(BF)
        near = with_neighbours(hidden)[:, :width]
        e = jnp.dot(w2_ref[...], near, preferred_element_type=jnp.float32)
        o_ref[k] = (c2[...] + e[2 * out :] + b2_ref[...]).astype(BF)
        c2[...] = a2[...] + e[out : 2 * out]
        a2[...] = e[:out] + (d[3 * out :, :width] + skip_ref[k])


def laid_out(kernel, shortcut):
    out, cin = shortcut.shape
    w = kernel.transpose(0, 2, 1, 3).reshape(3 * out, 3 * cin)
    skip = jnp.concatenate([jnp.zeros_like(shortcut), shortcut, jnp.zeros_like(shortcut)], axis=1)
    return jnp.concatenate([w, skip], axis=0)


def padded_to(w, size):
    return jnp.concatenate([w, jnp.zeros(w.shape[:-1] + (size - w.shape[-1],), w.dtype)], -1)


def of_groups(w, starts, share, size):
    parts, done = [], 0
    for start in starts:
        seen = min(max(done - start, 0), share)
        parts += [jnp.zeros(w.shape[:-1] + (seen,), w.dtype), w[..., start + seen : start + share]]
        done = max(done, start + share)
    return padded_to(jnp.concatenate(parts, -1), size)


def finish(cond, lon, part, skip, mask, w1, first_bias, w2, second_bias, width):
    tall, lanes = cond.shape[0], lon.shape[1]
    out = part.shape[1]
    rows, step_rows = tall - 4, 4
    whole = lambda shape: pl.BlockSpec(shape, lambda i: (0,) * len(shape))
    by_row = lambda x: pl.BlockSpec((step_rows,) + x.shape[1:], lambda i: (i, 0, 0))
    total = jax.ShapeDtypeStruct((rows, out, width), BF)
    return pl.pallas_call(
        functools.partial(finish_kernel, step_rows, rows, out),
        out_shape=total,
        grid=(tall // step_rows,),
        in_specs=[whole((1, lanes)), whole(lon.shape), by_row(cond), by_row(part), by_row(skip), whole(w1.shape), whole((out, 1)),
                  whole(w2.shape), whole((out, 1))],
        out_specs=pl.BlockSpec((step_rows, out, width), lambda i: (jnp.maximum(i - 1, 0), 0, 0)),
        scratch_shapes=[pltpu.VMEM((out, lanes), F32)] * 2 + [pltpu.VMEM((out, width), F32)] * 2,
        compiler_params=pltpu.CompilerParams(dimension_semantics=("arbitrary",), vmem_limit_bytes=60 << 20),
    )(mask, lon, cond, part, skip, w1, first_bias[:, None], w2, second_bias[:, None])


def denoise(state, cond, mask, place, first_kernel, first_bias, second_kernel, second_bias, shortcut, s_ch, width, starts, share):
    tall, s_pad, lanes = state.shape
    c_pad = cond.shape[1]
    out, cin = shortcut.shape
    rows = tall - 4
    step_rows = 4

    def spread(w):
        zero = lambda n: jnp.zeros(w.shape[:-1] + (n,), w.dtype)
        parts = [w[..., :s_ch], zero(s_pad - s_ch)]
        done = s_ch
        for start in starts:
            seen = min(max(done - (s_ch + start), 0), share)
            end = s_ch + start + share
            parts += [zero(seen), w[..., end - share + seen : end]]
            done = max(done, end)
        return jnp.concatenate(parts + [zero(c_pad - share * len(starts))], -1)

    w1 = spread(first_kernel).transpose(0, 2, 1, 3).reshape(3 * out, 3 * (s_pad + c_pad))
    skip = spread(shortcut)
    skip = jnp.concatenate([jnp.zeros_like(skip), skip, jnp.zeros_like(skip)], axis=1)
    w1 = jnp.concatenate([w1, skip], axis=0)
    w2 = second_kernel.transpose(0, 2, 1, 3).reshape(3 * out, 3 * out)
    whole = lambda shape: pl.BlockSpec(shape, lambda i: (0,) * len(shape))
    total = jax.ShapeDtypeStruct((rows, out, width), BF)
    scratch = pltpu.VMEM((out, lanes), jnp.float32)
    return pl.pallas_call(
        functools.partial(block_kernel, step_rows, out),
        out_shape=total,
        grid=(tall // step_rows,),
        in_specs=[
            pl.BlockSpec(memory_space=pltpu.SMEM),
            whole((1, lanes)),
            pl.BlockSpec((step_rows, s_pad, lanes), lambda i: (i, 0, 0)),
            pl.BlockSpec((step_rows, c_pad, lanes), lambda i: (i, 0, 0)),
            whole(w1.shape),
            whole((out, 1)),
            whole(w2.shape),
            whole((out, 1)),
        ],
        out_specs=pl.BlockSpec((step_rows, out, width), lambda i: (jnp.maximum(i - 1, 0), 0, 0)),
        scratch_shapes=[scratch] * 4,
        compiler_params=pltpu.CompilerParams(dimension_semantics=("arbitrary",)),
        cost_estimate=pl.CostEstimate(
            flops=2 * tall * lanes * (w1.size + w2.size),
            bytes_accessed=2 * (state.size + cond.size + total.size),
            transcendentals=tall * out * lanes,
        ),
    )(place, mask, state, cond, w1, first_bias[:, None], w2, second_bias[:, None])


def shards(
    global_field,
    regional_state,
    windows,
    longitude_weights,
    latitude_weights,
    first_kernel,
    first_bias,
    second_kernel,
    later_conv_bias,
    shortcut_weight,
):
    tiles = lax.axis_size("tile")
    regions = lax.axis_size("region")
    tile_index = lax.axis_index("tile")
    region_index = lax.axis_index("region")
    half = tiles // 2
    row_tiles = half // TCOLS
    rotation = tiles // 4 + 2
    position = (tile_index + rotation) % tiles
    domain_half = position // half
    within = position % half
    row_tile = within // TCOLS
    col_tile = within % TCOLS
    my_domain = 2 * region_index + domain_half
    state = regional_state[0]
    channels, rows, cols = state.shape
    field_channels = global_field.shape[0]

    lat_window, lon_window = latitude_weights.shape[2], longitude_weights.shape[2]
    share = -(-field_channels // tiles)
    starts = [owned_start(t, tiles, field_channels, share) for t in range(tiles)]
    out = shortcut_weight.shape[0]
    flat = state.transpose(1, 0, 2)
    fused = global_field.shape[1] == lat_window and row_tiles == 1
    if fused:
        s_pad, c_pad = channels + -channels % 16, tiles * share + -(tiles * share) % 16
        w_state = laid_out(padded_to(first_kernel[..., :channels], s_pad), padded_to(shortcut_weight[:, :channels], s_pad))
        w_cond = laid_out(
            of_groups(first_kernel[..., channels:], starts, share, c_pad),
            of_groups(shortcut_weight[:, channels:], starts, share, c_pad),
        )
        window, part, skip = exchange(
            global_field, windows, flat, w_state, region_index, lat_window, lon_window, rotation
        )
    else:
        window = exchange_by_collectives(global_field, windows, region_index, lat_window, lon_window, rotation)
        window = window.reshape((tiles * share,) + window.shape[2:])

    own = lax.dynamic_index_in_dim(windows, my_domain, 0, keepdims=False)
    lon = lax.dynamic_index_in_dim(longitude_weights, my_domain, 0, keepdims=False)
    lon = lon * (jnp.arange(lon.shape[1]) < own[3]).astype(BF)[None, :]
    lon = lax.dynamic_slice_in_dim(jnp.pad(lon, ((2, 2), (0, 0))), col_tile * cols, cols + 4, 0)
    lat = lax.dynamic_index_in_dim(latitude_weights, domain_half, 0, keepdims=False)
    lat = lat * (jnp.arange(lat.shape[1]) < own[1]).astype(BF)[None, :]
    lat = lax.dynamic_slice_in_dim(jnp.pad(lat, ((2, 2), (0, 0))), row_tile * rows, rows + 4, 0)
    lat = jnp.roll(lat, own[0] % lat.shape[1], axis=1)

    lanes = 2 * cols
    lon = around(lon.T, lanes)
    x = around(jnp.arange(-2, cols + 2) + col_tile * cols + 1, lanes) - 1
    mask = ((x >= 0) & (x < TCOLS * cols)).astype(F32)[None, :]
    if fused:
        w2 = second_kernel.transpose(0, 2, 1, 3).reshape(3 * out, 3 * out)
        rowed = jnp.einsum("yl,clk->yck", lat, window, preferred_element_type=F32).astype(BF)
        result = finish(rowed, lon, part, skip, mask, w_cond, first_bias, w2, later_conv_bias, cols)
        return result.transpose(1, 0, 2)[None]

    bands = jnp.einsum("clk,kx->clx", window, lon, preferred_element_type=F32).astype(BF)
    condition = jnp.einsum("yl,clx->ycx", lat, bands, preferred_element_type=F32).astype(BF)
    condition = jnp.pad(condition, ((0, 0), (0, -condition.shape[1] % 16), (0, 0)))

    left = passed_along(flat[:, :, cols - 2 :], "tile", 1) * (col_tile > 0).astype(BF)
    right = passed_along(flat[:, :, :2], "tile", -1) * (col_tile < TCOLS - 1).astype(BF)
    wide = around(jnp.concatenate([left, flat, right], axis=2), lanes)
    if row_tiles > 1:
        above = passed_along(wide[rows - 2 :], "tile", TCOLS) * (row_tile > 0).astype(BF)
        below = passed_along(wide[:2], "tile", -TCOLS) * (row_tile < row_tiles - 1).astype(BF)
        wide = jnp.concatenate([above, wide, below], axis=0)
        wide = jnp.pad(wide, ((0, 0), (0, -channels % 16), (0, 0)))
    else:
        wide = jnp.pad(wide, ((2, 2), (0, -channels % 16), (0, 0)))

    place = jnp.stack([row_tile * rows, row_tiles * rows]).astype(jnp.int32)
    result = denoise(
        wide, condition, mask, place, first_kernel, first_bias, second_kernel, later_conv_bias, shortcut_weight,
        channels, cols, starts, share,
    )
    return result.transpose(1, 0, 2)[None]


def solution(mesh):
    placed = (
        P(None, "tile", "region"),
        P(("region", "tile"), None, None, None),
        P(),
        P(),
        P("region", None, None),
        P(),
        P(),
        P(),
        P(),
        P(),
    )
    return jax.shard_map(
        shards,
        mesh=mesh,
        in_specs=placed,
        out_specs=P(("region", "tile"), None, None, None),
        check_vma=False,
    )
```

```python
import functools

import jax
import jax.numpy as jnp
from jax import lax
from jax.experimental import pallas as pl
from jax.experimental.pallas import tpu as pltpu
from jax.sharding import PartitionSpec as P

TCOLS = 4
BF = jnp.bfloat16
F32 = jnp.float32
MESH = pl.DeviceIdType.MESH


def passed_along(block, axis, distance):
    devices = range(lax.axis_size(axis))
    route = [((i - distance) % len(devices), i) for i in devices]
    return lax.ppermute(block, axis, route)


def windows_of_domains(field, windows, region_index, lat_window, lon_window):
    tiles = lax.axis_size("tile")
    channels, band, cols = field.shape
    share = -(-channels // tiles)
    starts = [owned_start(t, tiles, channels, share) for t in range(tiles)]
    split = jnp.stack([field[start : start + share] for start in starts])
    bands = lax.all_to_all(split, "tile", split_axis=0, concat_axis=0, tiled=True)
    per = lat_window // band
    groups = bands.reshape(tiles // per, per, share, band, cols)
    groups = groups.transpose(0, 2, 1, 3, 4).reshape(tiles // per, share, lat_window, cols)
    count = groups.shape[0]
    row = jnp.arange(lat_window)[None, :, None]
    col = jnp.arange(cols)[:, None] + region_index * cols
    pieces = []
    for domain in range(windows.shape[0]):
        group, shift = windows[domain, 0] // lat_window, windows[domain, 0] % lat_window
        here = lax.dynamic_index_in_dim(groups, group, 0, keepdims=False)
        following = lax.dynamic_index_in_dim(groups, jnp.minimum(group + 1, count - 1), 0, keepdims=False)
        rows = jnp.where(row >= shift, here, following)
        pick = (col == jnp.arange(lon_window)[None, :] + windows[domain, 2]).astype(BF)
        pieces.append(jnp.einsum("clj,jk->clk", rows, pick, preferred_element_type=F32).astype(BF))
    return jnp.stack(pieces)


def owned_start(peer, tiles, channels, share):
    return peer * (channels - share) // (tiles - 1)


def exchange_kernel(
    sizes, windows_ref, field_ref, pick_ref, state_ref, w_ref, o_ref, part_out, skip_out,
    got1, send2, got2, send3, s1, r1, own1, s2, r2, s3, r3, edges, sides, padded, a1, c1, s4, r4, part_ref, skip_ref, leave1, leave2,
):
    tiles, regions, channels, share, chunk, lat_window, rotation = sizes
    me, region = lax.axis_index("tile"), lax.axis_index("region")
    chunks, half = share // chunk, tiles // 2
    domains = 2 * regions

    def tile_peer(p):
        return lax.rem(me + p, tiles)

    def region_peer(p):
        return lax.rem(region + p, regions)

    rows, s_ch, width = state_ref.shape
    out = part_ref.shape[1]
    lane = lax.broadcasted_iota(jnp.int32, (s_ch, width), 1)
    column = lax.rem(lax.rem(me + rotation, tiles), TCOLS)

    def edge(side):
        peer = tile_peer(1 if side == 0 else tiles - 1)
        return pltpu.make_async_remote_copy(
            src_ref=edges.at[side], dst_ref=sides.at[side], send_sem=s4.at[side], recv_sem=r4.at[side],
            device_id=(region, peer), device_id_type=MESH,
        )

    barrier = pltpu.get_barrier_semaphore()
    for p in range(1, tiles):
        pl.semaphore_signal(barrier, inc=1, device_id=(region, tile_peer(p)), device_id_type=MESH)
    for p in range(1, regions):
        pl.semaphore_signal(barrier, inc=1, device_id=(region_peer(p), me), device_id_type=MESH)
    edges[...] = jnp.zeros_like(edges)

    def pack(y, packed):
        row = state_ref[y].astype(F32)
        last, first_two = packed
        here = (lane >= 2 * y) & (lane < 2 * y + 2)
        last = jnp.where(here, pltpu.roll(row, lax.rem(2 * y + 2, width), 1), last)
        first_two = jnp.where(here, pltpu.roll(row, 2 * y, 1), first_two)
        return last, first_two

    zero = jnp.zeros((s_ch, width), F32)
    last, first_two = lax.fori_loop(0, rows, pack, (zero, zero))
    edges[0, :s_ch] = last.astype(BF)
    edges[1, :s_ch] = first_two.astype(BF)
    padded[...] = jnp.zeros_like(padded)
    a1[...] = jnp.zeros_like(a1)
    c1[...] = jnp.zeros_like(c1)
    pl.semaphore_wait(barrier, tiles + regions - 2)
    for side in range(2):
        edge(side).start()

    def first(k, p):
        peer = tile_peer(p)
        start = owned_start(peer, tiles, channels, share) + k * chunk
        return pltpu.make_async_remote_copy(
            src_ref=field_ref.at[pl.ds(start, chunk)], dst_ref=got1[k].at[me], send_sem=s1.at[k, peer],
            recv_sem=r1.at[k, me], device_id=(region, peer), device_id_type=MESH,
        )

    def first_from(k, p):
        peer = tile_peer(p)
        return pltpu.make_async_remote_copy(
            src_ref=got1[k].at[peer], dst_ref=got1[k].at[peer], send_sem=s1.at[k, peer],
            recv_sem=r1.at[k, peer], device_id=(region, peer), device_id_type=MESH,
        )

    def keep(k):
        start = owned_start(me, tiles, channels, share) + k * chunk
        return pltpu.make_async_copy(field_ref.at[pl.ds(start, chunk)], got1[k].at[me], own1.at[k])

    def second(k, p, source):
        peer = region_peer(p)
        return pltpu.make_async_remote_copy(
            src_ref=send2.at[k, peer], dst_ref=got2.at[k, peer if source else region], send_sem=s2.at[k, peer],
            recv_sem=r2.at[k, peer if source else region], device_id=(peer, me), device_id_type=MESH,
        )

    def third(k, p, source):
        peer = tile_peer(p)
        part = (lax.rem(peer + rotation, tiles)) // half
        return pltpu.make_async_remote_copy(
            src_ref=send3.at[k, part], dst_ref=o_ref.at[pl.ds((peer if source else me) * share + k * chunk, chunk)],
            send_sem=s3.at[k, peer], recv_sem=r3.at[k, peer if source else me],
            device_id=(region, peer), device_id_type=MESH,
        )

    for k in range(chunks):
        keep(k).start()
        for p in range(1, tiles):
            first(k, p).start()

    cuts = [rows * n // (chunks + 1) // 2 * 2 for n in range(chunks + 1)] + [rows]

    def state_rows(begin, end):
        lane_f = lax.broadcasted_iota(jnp.int32, (padded.shape[0], width), 1)

        def one(y, _):
            padded[:s_ch] = state_ref[y]
            after = pltpu.roll(sides[1].astype(F32), lax.rem(width - 2 * y, width), 1)
            before = pltpu.roll(sides[0].astype(F32), lax.rem(2 * width - 2 - 2 * y, width), 1)
            halo = jnp.where((lane_f < 2) & (column < TCOLS - 1), after, 0.0)
            halo = jnp.where((lane_f >= width - 2) & (column > 0), before, halo)
            row = jnp.concatenate([padded[...], halo.astype(BF)], axis=1)
            d = jnp.dot(w_ref[...], with_neighbours(row), preferred_element_type=F32)
            part_ref[y + 2] = c1[...] + d[2 * out : 3 * out]
            c1[...] = a1[...] + d[out : 2 * out]
            a1[...] = d[:out]
            skip_ref[y + 2] = d[3 * out :, :width]
            return 0

        lax.fori_loop(begin, end, one, 0, unroll=2)

    def leave(n):
        begin, end = cuts[n] + 2, cuts[n + 1] + (3 if n == chunks else 2)
        span = pl.ds(begin, end - begin)
        return (
            pltpu.make_async_copy(part_ref.at[span], part_out.at[span], leave1.at[n]),
            pltpu.make_async_copy(skip_ref.at[span], skip_out.at[span], leave2.at[n]),
        )

    def extract(k):
        for p in range(1, tiles):
            first_from(k, p).wait_recv()
        keep(k).wait()
        cols = pick_ref.shape[1]
        row = lax.broadcasted_iota(jnp.int32, (chunk, lat_window, cols), 1)
        for d in range(domains):
            group, shift = windows_ref[d, 0] // lat_window, lax.rem(windows_ref[d, 0], lat_window)
            here = got1[k][group]
            following = got1[k][jnp.minimum(group + 1, tiles - 1)]
            rows = jnp.where(row >= shift, here.astype(F32), following.astype(F32)).astype(BF)
            found = jnp.dot(rows.reshape(chunk * lat_window, cols), pick_ref[d], preferred_element_type=F32)
            send2[k, d // 2, d % 2] = found.astype(BF).reshape(chunk, lat_window, found.shape[1])
        got2[k, region] = send2[k, region]
        for p in range(1, regions):
            second(k, p, False).start()

    def combine(k):
        for p in range(1, regions):
            second(k, p, True).wait_recv()
        total = got2[k, 0]
        for r in range(1, regions):
            total = total + got2[k, r]
        send3[k] = total
        for p in range(1, tiles):
            third(k, p, False).start()
        o_ref[pl.ds(me * share + k * chunk, chunk)] = send3[k, lax.rem(me + rotation, tiles) // half]

    o_ref[tiles * share :] = jnp.zeros_like(o_ref[tiles * share :])
    for side in range(2):
        edge(side).wait_recv()
    for k in range(chunks):
        state_rows(cuts[k], cuts[k + 1])
        for copy in leave(k):
            copy.start()
        extract(k)
        if k > 0:
            combine(k - 1)
    state_rows(cuts[chunks], rows)
    part_ref[rows + 2] = c1[...]
    skip_ref[rows + 2] = jnp.zeros(skip_ref.shape[1:], F32)
    for copy in leave(chunks):
        copy.start()
    combine(chunks - 1)
    for k in range(chunks):
        for p in range(1, tiles):
            third(k, p, True).wait_recv()
    for n in range(chunks + 1):
        for copy in leave(n):
            copy.wait()
    for side in range(2):
        edge(side).wait_send()
    for k in range(chunks):
        for p in range(1, tiles):
            first(k, p).wait_send()
            third(k, p, False).wait_send()
        for p in range(1, regions):
            second(k, p, False).wait_send()


def exchange(field, windows, state, weights, region_index, lat_window, lon_window, rotation):
    tiles, regions = lax.axis_size("tile"), lax.axis_size("region")
    channels, band, cols = field.shape
    share = -(-channels // tiles)
    chunk = 1
    chunks = share // chunk
    rows, s_ch, width = state.shape
    out, s_pad = weights.shape[0] // 4, weights.shape[1] // 3
    held = tiles * share + -(tiles * share) % 16
    col = jnp.arange(cols)[None, :, None] + region_index * cols
    pick = (col == jnp.arange(lon_window)[None, None, :] + windows[:, 2][:, None, None]).astype(BF)
    vmem = pl.BlockSpec(memory_space=pltpu.VMEM)
    block = (chunk, lat_window, lon_window)
    dma = pltpu.SemaphoreType.DMA
    return pl.pallas_call(
        functools.partial(exchange_kernel, (tiles, regions, channels, share, chunk, lat_window, rotation)),
        out_shape=(
            jax.ShapeDtypeStruct((held, lat_window, lon_window), BF),
            jax.ShapeDtypeStruct((rows + 4, out, 2 * width), F32),
            jax.ShapeDtypeStruct((rows + 4, out, width), F32),
        ),
        in_specs=[pl.BlockSpec(memory_space=pltpu.SMEM), pl.BlockSpec(memory_space=pl.ANY), vmem, vmem, vmem],
        out_specs=(vmem, pl.BlockSpec(memory_space=pl.ANY), pl.BlockSpec(memory_space=pl.ANY)),
        scratch_shapes=[
            [pltpu.VMEM((tiles, chunk, band, cols), BF)] * chunks,
            pltpu.VMEM((chunks, regions, 2) + block, BF),
            pltpu.VMEM((chunks, regions, 2) + block, BF),
            pltpu.VMEM((chunks, 2) + block, BF),
            dma((chunks, tiles)),
            dma((chunks, tiles)),
            dma((chunks,)),
            dma((chunks, regions)),
            dma((chunks, regions)),
            dma((chunks, tiles)),
            dma((chunks, tiles)),
            pltpu.VMEM((2, s_pad, width), BF),
            pltpu.VMEM((2, s_pad, width), BF),
            pltpu.VMEM((s_pad, width), BF),
            pltpu.VMEM((out, 2 * width), F32),
            pltpu.VMEM((out, 2 * width), F32),
            dma((2,)),
            dma((2,)),
            pltpu.VMEM((rows + 4, out, 2 * width), F32),
            pltpu.VMEM((rows + 4, out, width), F32),
            dma((chunks + 1,)),
            dma((chunks + 1,)),
        ],
        compiler_params=pltpu.CompilerParams(collective_id=0, has_side_effects=True, vmem_limit_bytes=60 << 20),
    )(windows, field, pick, state, weights)


def exchange_by_collectives(field, windows, region_index, lat_window, lon_window, rotation):
    tiles, regions = lax.axis_size("tile"), lax.axis_size("region")
    pieces = windows_of_domains(field, windows, region_index, lat_window, lon_window)
    sent = pieces.reshape((regions, 2) + pieces.shape[1:])
    got = lax.all_to_all(sent, "region", split_axis=0, concat_axis=0, tiled=True)
    mine = got.astype(F32).sum(0).astype(BF)
    halves = [((t + rotation) % tiles) // (tiles // 2) for t in range(tiles)]
    spread = jnp.stack([mine[h] for h in halves])
    return lax.all_to_all(spread, "tile", split_axis=0, concat_axis=0, tiled=True)


def around(value, lanes):
    zeros = jnp.zeros(value.shape[:-1] + (lanes - value.shape[-1],), value.dtype)
    return jnp.concatenate([value[..., 2:], zeros, value[..., :2]], axis=-1)


def with_neighbours(value):
    return jnp.concatenate([pltpu.roll(value, 1, 1), value, pltpu.roll(value, value.shape[1] - 1, 1)], axis=0)


def block_kernel(step_rows, out, place, mask_ref, state_ref, cond_ref, w1_ref, b1_ref, w2_ref, b2_ref, o_ref, a1, c1, a2, c2):
    step = pl.program_id(0)

    @pl.when(step == 0)
    def _():
        for ref in (a1, c1, a2, c2):
            ref[...] = jnp.zeros_like(ref)

    width = o_ref.shape[2]
    mask = mask_ref[...] > 0
    for k in range(step_rows):
        row = jnp.concatenate([state_ref[k], cond_ref[k]], axis=0)
        d = jnp.dot(w1_ref[...], with_neighbours(row), preferred_element_type=jnp.float32)
        full = c1[...] + d[2 * out : 3 * out] + b1_ref[...]
        c1[...] = a1[...] + d[out : 2 * out]
        a1[...] = d[:out]
        y = step * step_rows + k - 3 + place[0]
        inside = mask & (y >= 0) & (y < place[1])
        hidden = jnp.where(inside, full / (1.0 + jnp.exp(-full)), 0.0).astype(BF)
        e = jnp.dot(w2_ref[...], with_neighbours(hidden), preferred_element_type=jnp.float32)
        o_ref[k] = (c2[...] + e[2 * out :] + b2_ref[...])[:, :width].astype(BF)
        c2[...] = a2[...] + e[out : 2 * out]
        a2[...] = e[:out] + d[3 * out :]


def finish_kernel(step_rows, rows, out, mask_ref, cond_ref, part_ref, skip_ref, w1_ref, b1_ref, w2_ref, b2_ref, o_ref, a1, c1, a2, c2):
    step = pl.program_id(0)

    @pl.when(step == 0)
    def _():
        for ref in (a1, c1, a2, c2):
            ref[...] = jnp.zeros_like(ref)

    width = o_ref.shape[2]
    mask = mask_ref[...] > 0
    for k in range(step_rows):
        d = jnp.dot(w1_ref[...], with_neighbours(cond_ref[k]), preferred_element_type=jnp.float32)
        full = c1[...] + d[2 * out : 3 * out] + (part_ref[k] + b1_ref[...])
        c1[...] = a1[...] + d[out : 2 * out]
        a1[...] = d[:out]
        y = step * step_rows + k - 3
        inside = mask & (y >= 0) & (y < rows)
        hidden = jnp.where(inside, full / (1.0 + jnp.exp(-full)), 0.0).astype(BF)
        near = with_neighbours(hidden)[:, :width]
        e = jnp.dot(w2_ref[...], near, preferred_element_type=jnp.float32)
        o_ref[k] = (c2[...] + e[2 * out :] + b2_ref[...]).astype(BF)
        c2[...] = a2[...] + e[out : 2 * out]
        a2[...] = e[:out] + (d[3 * out :, :width] + skip_ref[k])


def laid_out(kernel, shortcut):
    out, cin = shortcut.shape
    w = kernel.transpose(0, 2, 1, 3).reshape(3 * out, 3 * cin)
    skip = jnp.concatenate([jnp.zeros_like(shortcut), shortcut, jnp.zeros_like(shortcut)], axis=1)
    return jnp.concatenate([w, skip], axis=0)


def padded_to(w, size):
    return jnp.concatenate([w, jnp.zeros(w.shape[:-1] + (size - w.shape[-1],), w.dtype)], -1)


def of_groups(w, starts, share, size):
    parts, done = [], 0
    for start in starts:
        seen = min(max(done - start, 0), share)
        parts += [jnp.zeros(w.shape[:-1] + (seen,), w.dtype), w[..., start + seen : start + share]]
        done = max(done, start + share)
    return padded_to(jnp.concatenate(parts, -1), size)


def finish(cond, part, skip, mask, w1, first_bias, w2, second_bias, width):
    tall, lanes = cond.shape[0], cond.shape[2]
    part, skip = (pltpu.with_memory_space_constraint(v, pltpu.HBM) for v in (part, skip))
    out = part.shape[1]
    rows, step_rows = tall - 4, 4
    whole = lambda shape: pl.BlockSpec(shape, lambda i: (0,) * len(shape))
    by_row = lambda x: pl.BlockSpec((step_rows,) + x.shape[1:], lambda i: (i, 0, 0))
    total = jax.ShapeDtypeStruct((rows, out, width), BF)
    return pl.pallas_call(
        functools.partial(finish_kernel, step_rows, rows, out),
        out_shape=total,
        grid=(tall // step_rows,),
        in_specs=[whole((1, lanes)), by_row(cond), by_row(part), by_row(skip), whole(w1.shape), whole((out, 1)),
                  whole(w2.shape), whole((out, 1))],
        out_specs=pl.BlockSpec((step_rows, out, width), lambda i: (jnp.maximum(i - 1, 0), 0, 0)),
        scratch_shapes=[pltpu.VMEM((out, lanes), F32)] * 2 + [pltpu.VMEM((out, width), F32)] * 2,
        compiler_params=pltpu.CompilerParams(dimension_semantics=("arbitrary",), vmem_limit_bytes=40 << 20),
    )(mask, cond, part, skip, w1, first_bias[:, None], w2, second_bias[:, None])


def denoise(state, cond, mask, place, first_kernel, first_bias, second_kernel, second_bias, shortcut, s_ch, width, starts, share):
    tall, s_pad, lanes = state.shape
    c_pad = cond.shape[1]
    out, cin = shortcut.shape
    rows = tall - 4
    step_rows = 4

    def spread(w):
        zero = lambda n: jnp.zeros(w.shape[:-1] + (n,), w.dtype)
        parts = [w[..., :s_ch], zero(s_pad - s_ch)]
        done = s_ch
        for start in starts:
            seen = min(max(done - (s_ch + start), 0), share)
            end = s_ch + start + share
            parts += [zero(seen), w[..., end - share + seen : end]]
            done = max(done, end)
        return jnp.concatenate(parts + [zero(c_pad - share * len(starts))], -1)

    w1 = spread(first_kernel).transpose(0, 2, 1, 3).reshape(3 * out, 3 * (s_pad + c_pad))
    skip = spread(shortcut)
    skip = jnp.concatenate([jnp.zeros_like(skip), skip, jnp.zeros_like(skip)], axis=1)
    w1 = jnp.concatenate([w1, skip], axis=0)
    w2 = second_kernel.transpose(0, 2, 1, 3).reshape(3 * out, 3 * out)
    whole = lambda shape: pl.BlockSpec(shape, lambda i: (0,) * len(shape))
    total = jax.ShapeDtypeStruct((rows, out, width), BF)
    scratch = pltpu.VMEM((out, lanes), jnp.float32)
    return pl.pallas_call(
        functools.partial(block_kernel, step_rows, out),
        out_shape=total,
        grid=(tall // step_rows,),
        in_specs=[
            pl.BlockSpec(memory_space=pltpu.SMEM),
            whole((1, lanes)),
            pl.BlockSpec((step_rows, s_pad, lanes), lambda i: (i, 0, 0)),
            pl.BlockSpec((step_rows, c_pad, lanes), lambda i: (i, 0, 0)),
            whole(w1.shape),
            whole((out, 1)),
            whole(w2.shape),
            whole((out, 1)),
        ],
        out_specs=pl.BlockSpec((step_rows, out, width), lambda i: (jnp.maximum(i - 1, 0), 0, 0)),
        scratch_shapes=[scratch] * 4,
        compiler_params=pltpu.CompilerParams(dimension_semantics=("arbitrary",)),
        cost_estimate=pl.CostEstimate(
            flops=2 * tall * lanes * (w1.size + w2.size),
            bytes_accessed=2 * (state.size + cond.size + total.size),
            transcendentals=tall * out * lanes,
        ),
    )(place, mask, state, cond, w1, first_bias[:, None], w2, second_bias[:, None])


def shards(
    global_field,
    regional_state,
    windows,
    longitude_weights,
    latitude_weights,
    first_kernel,
    first_bias,
    second_kernel,
    later_conv_bias,
    shortcut_weight,
):
    tiles = lax.axis_size("tile")
    regions = lax.axis_size("region")
    tile_index = lax.axis_index("tile")
    region_index = lax.axis_index("region")
    half = tiles // 2
    row_tiles = half // TCOLS
    rotation = tiles // 4 + 2
    position = (tile_index + rotation) % tiles
    domain_half = position // half
    within = position % half
    row_tile = within // TCOLS
    col_tile = within % TCOLS
    my_domain = 2 * region_index + domain_half
    state = regional_state[0]
    channels, rows, cols = state.shape
    field_channels = global_field.shape[0]

    lat_window, lon_window = latitude_weights.shape[2], longitude_weights.shape[2]
    share = -(-field_channels // tiles)
    starts = [owned_start(t, tiles, field_channels, share) for t in range(tiles)]
    out = shortcut_weight.shape[0]
    flat = state.transpose(1, 0, 2)
    fused = global_field.shape[1] == lat_window and row_tiles == 1
    if fused:
        s_pad, c_pad = channels + -channels % 16, tiles * share + -(tiles * share) % 16
        w_state = laid_out(padded_to(first_kernel[..., :channels], s_pad), padded_to(shortcut_weight[:, :channels], s_pad))
        w_cond = laid_out(
            of_groups(first_kernel[..., channels:], starts, share, c_pad),
            of_groups(shortcut_weight[:, channels:], starts, share, c_pad),
        )
        window, part, skip = exchange(
            global_field, windows, flat, w_state, region_index, lat_window, lon_window, rotation
        )
    else:
        window = exchange_by_collectives(global_field, windows, region_index, lat_window, lon_window, rotation)
        window = window.reshape((tiles * share,) + window.shape[2:])

    own = lax.dynamic_index_in_dim(windows, my_domain, 0, keepdims=False)
    lon = lax.dynamic_index_in_dim(longitude_weights, my_domain, 0, keepdims=False)
    lon = lon * (jnp.arange(lon.shape[1]) < own[3]).astype(BF)[None, :]
    lon = lax.dynamic_slice_in_dim(jnp.pad(lon, ((2, 2), (0, 0))), col_tile * cols, cols + 4, 0)
    lat = lax.dynamic_index_in_dim(latitude_weights, domain_half, 0, keepdims=False)
    lat = lat * (jnp.arange(lat.shape[1]) < own[1]).astype(BF)[None, :]
    lat = lax.dynamic_slice_in_dim(jnp.pad(lat, ((2, 2), (0, 0))), row_tile * rows, rows + 4, 0)
    lat = jnp.roll(lat, own[0] % lat.shape[1], axis=1)

    lanes = 2 * cols
    lon = around(lon.T, lanes)
    bands = jnp.einsum("clk,kx->clx", window, lon, preferred_element_type=F32).astype(BF)
    condition = jnp.einsum("yl,clx->ycx", lat, bands, preferred_element_type=F32).astype(BF)
    x = around(jnp.arange(-2, cols + 2) + col_tile * cols + 1, lanes) - 1
    mask = ((x >= 0) & (x < TCOLS * cols)).astype(F32)[None, :]
    if fused:
        w2 = second_kernel.transpose(0, 2, 1, 3).reshape(3 * out, 3 * out)
        result = finish(condition, part, skip, mask, w_cond, first_bias, w2, later_conv_bias, cols)
        return result.transpose(1, 0, 2)[None]

    condition = jnp.pad(condition, ((0, 0), (0, -condition.shape[1] % 16), (0, 0)))
    left = passed_along(flat[:, :, cols - 2 :], "tile", 1) * (col_tile > 0).astype(BF)
    right = passed_along(flat[:, :, :2], "tile", -1) * (col_tile < TCOLS - 1).astype(BF)
    wide = around(jnp.concatenate([left, flat, right], axis=2), lanes)
    if row_tiles > 1:
        above = passed_along(wide[rows - 2 :], "tile", TCOLS) * (row_tile > 0).astype(BF)
        below = passed_along(wide[:2], "tile", -TCOLS) * (row_tile < row_tiles - 1).astype(BF)
        wide = jnp.concatenate([above, wide, below], axis=0)
        wide = jnp.pad(wide, ((0, 0), (0, -channels % 16), (0, 0)))
    else:
        wide = jnp.pad(wide, ((2, 2), (0, -channels % 16), (0, 0)))

    place = jnp.stack([row_tile * rows, row_tiles * rows]).astype(jnp.int32)
    result = denoise(
        wide, condition, mask, place, first_kernel, first_bias, second_kernel, later_conv_bias, shortcut_weight,
        channels, cols, starts, share,
    )
    return result.transpose(1, 0, 2)[None]


def solution(mesh):
    placed = (
        P(None, "tile", "region"),
        P(("region", "tile"), None, None, None),
        P(),
        P(),
        P("region", None, None),
        P(),
        P(),
        P(),
        P(),
        P(),
    )
    return jax.shard_map(
        shards,
        mesh=mesh,
        in_specs=placed,
        out_specs=P(("region", "tile"), None, None, None),
        check_vma=False,
    )
```

```python
import functools

import jax
import jax.numpy as jnp
from jax import lax
from jax.experimental import pallas as pl
from jax.experimental.pallas import tpu as pltpu
from jax.sharding import PartitionSpec as P

TCOLS = 4
BF = jnp.bfloat16
F32 = jnp.float32
MESH = pl.DeviceIdType.MESH


def passed_along(block, axis, distance):
    devices = range(lax.axis_size(axis))
    route = [((i - distance) % len(devices), i) for i in devices]
    return lax.ppermute(block, axis, route)


def windows_of_domains(field, windows, region_index, lat_window, lon_window):
    tiles = lax.axis_size("tile")
    channels, band, cols = field.shape
    share = -(-channels // tiles)
    starts = [owned_start(t, tiles, channels, share) for t in range(tiles)]
    split = jnp.stack([field[start : start + share] for start in starts])
    bands = lax.all_to_all(split, "tile", split_axis=0, concat_axis=0, tiled=True)
    per = lat_window // band
    groups = bands.reshape(tiles // per, per, share, band, cols)
    groups = groups.transpose(0, 2, 1, 3, 4).reshape(tiles // per, share, lat_window, cols)
    count = groups.shape[0]
    row = jnp.arange(lat_window)[None, :, None]
    col = jnp.arange(cols)[:, None] + region_index * cols
    pieces = []
    for domain in range(windows.shape[0]):
        group, shift = windows[domain, 0] // lat_window, windows[domain, 0] % lat_window
        here = lax.dynamic_index_in_dim(groups, group, 0, keepdims=False)
        following = lax.dynamic_index_in_dim(groups, jnp.minimum(group + 1, count - 1), 0, keepdims=False)
        rows = jnp.where(row >= shift, here, following)
        pick = (col == jnp.arange(lon_window)[None, :] + windows[domain, 2]).astype(BF)
        pieces.append(jnp.einsum("clj,jk->clk", rows, pick, preferred_element_type=F32).astype(BF))
    return jnp.stack(pieces)


def owned_start(peer, tiles, channels, share):
    return peer * (channels - share) // (tiles - 1)


def exchange_kernel(
    sizes, windows_ref, field_ref, pick_ref, state_ref, w_ref, o_ref, part_out, skip_out,
    got1, send2, got2, send3, s1, r1, own1, s2, r2, s3, r3, edges, sides, padded, a1, c1, s4, r4, part_ref, skip_ref, leave1, leave2,
):
    tiles, regions, channels, share, chunk, lat_window, rotation = sizes
    me, region = lax.axis_index("tile"), lax.axis_index("region")
    chunks, half = share // chunk, tiles // 2
    domains = 2 * regions

    def tile_peer(p):
        return lax.rem(me + p, tiles)

    def region_peer(p):
        return lax.rem(region + p, regions)

    rows, s_ch, width = state_ref.shape
    out = part_ref.shape[1]
    lane = lax.broadcasted_iota(jnp.int32, (s_ch, width), 1)
    column = lax.rem(lax.rem(me + rotation, tiles), TCOLS)

    def edge(side):
        peer = tile_peer(1 if side == 0 else tiles - 1)
        return pltpu.make_async_remote_copy(
            src_ref=edges.at[side], dst_ref=sides.at[side], send_sem=s4.at[side], recv_sem=r4.at[side],
            device_id=(region, peer), device_id_type=MESH,
        )

    barrier = pltpu.get_barrier_semaphore()
    for p in range(1, tiles):
        pl.semaphore_signal(barrier, inc=1, device_id=(region, tile_peer(p)), device_id_type=MESH)
    for p in range(1, regions):
        pl.semaphore_signal(barrier, inc=1, device_id=(region_peer(p), me), device_id_type=MESH)
    edges[...] = jnp.zeros_like(edges)

    def pack(y, packed):
        row = state_ref[y].astype(F32)
        last, first_two = packed
        here = (lane >= 2 * y) & (lane < 2 * y + 2)
        last = jnp.where(here, pltpu.roll(row, lax.rem(2 * y + 2, width), 1), last)
        first_two = jnp.where(here, pltpu.roll(row, 2 * y, 1), first_two)
        return last, first_two

    zero = jnp.zeros((s_ch, width), F32)
    last, first_two = lax.fori_loop(0, rows, pack, (zero, zero))
    edges[0, :s_ch] = last.astype(BF)
    edges[1, :s_ch] = first_two.astype(BF)
    padded[...] = jnp.zeros_like(padded)
    a1[...] = jnp.zeros_like(a1)
    c1[...] = jnp.zeros_like(c1)
    pl.semaphore_wait(barrier, tiles + regions - 2)
    for side in range(2):
        edge(side).start()

    def first(k, p):
        peer = tile_peer(p)
        start = owned_start(peer, tiles, channels, share) + k * chunk
        return pltpu.make_async_remote_copy(
            src_ref=field_ref.at[pl.ds(start, chunk)], dst_ref=got1[k].at[me], send_sem=s1.at[k, peer],
            recv_sem=r1.at[k, me], device_id=(region, peer), device_id_type=MESH,
        )

    def first_from(k, p):
        peer = tile_peer(p)
        return pltpu.make_async_remote_copy(
            src_ref=got1[k].at[peer], dst_ref=got1[k].at[peer], send_sem=s1.at[k, peer],
            recv_sem=r1.at[k, peer], device_id=(region, peer), device_id_type=MESH,
        )

    def keep(k):
        start = owned_start(me, tiles, channels, share) + k * chunk
        return pltpu.make_async_copy(field_ref.at[pl.ds(start, chunk)], got1[k].at[me], own1.at[k])

    def second(k, p, source):
        peer = region_peer(p)
        return pltpu.make_async_remote_copy(
            src_ref=send2.at[k, peer], dst_ref=got2.at[k, peer if source else region], send_sem=s2.at[k, peer],
            recv_sem=r2.at[k, peer if source else region], device_id=(peer, me), device_id_type=MESH,
        )

    def third(k, p, source):
        peer = tile_peer(p)
        part = (lax.rem(peer + rotation, tiles)) // half
        return pltpu.make_async_remote_copy(
            src_ref=send3.at[k, part], dst_ref=o_ref.at[pl.ds((peer if source else me) * share + k * chunk, chunk)],
            send_sem=s3.at[k, peer], recv_sem=r3.at[k, peer if source else me],
            device_id=(region, peer), device_id_type=MESH,
        )

    for k in range(chunks):
        keep(k).start()
        for p in range(1, tiles):
            first(k, p).start()

    cuts = [rows * n // (chunks + 1) // 2 * 2 for n in range(chunks + 1)] + [rows]

    def state_rows(begin, end):
        lane_f = lax.broadcasted_iota(jnp.int32, (padded.shape[0], width), 1)

        def one(y, _):
            padded[:s_ch] = state_ref[y]
            after = pltpu.roll(sides[1].astype(F32), lax.rem(width - 2 * y, width), 1)
            before = pltpu.roll(sides[0].astype(F32), lax.rem(2 * width - 2 - 2 * y, width), 1)
            halo = jnp.where((lane_f < 2) & (column < TCOLS - 1), after, 0.0)
            halo = jnp.where((lane_f >= width - 2) & (column > 0), before, halo)
            row = jnp.concatenate([padded[...], halo.astype(BF)], axis=1)
            d = jnp.dot(w_ref[...], with_neighbours(row), preferred_element_type=F32)
            part_ref[y + 2] = c1[...] + d[2 * out : 3 * out]
            c1[...] = a1[...] + d[out : 2 * out]
            a1[...] = d[:out]
            skip_ref[y + 2] = d[3 * out :, :width]
            return 0

        lax.fori_loop(begin, end, one, 0, unroll=2)

    def leave(n):
        begin, end = cuts[n] + 2, cuts[n + 1] + (3 if n == chunks else 2)
        span = pl.ds(begin, end - begin)
        return (
            pltpu.make_async_copy(part_ref.at[span], part_out.at[span], leave1.at[n]),
            pltpu.make_async_copy(skip_ref.at[span], skip_out.at[span], leave2.at[n]),
        )

    def extract(k):
        for p in range(1, tiles):
            first_from(k, p).wait_recv()
        keep(k).wait()
        cols = pick_ref.shape[1]
        row = lax.broadcasted_iota(jnp.int32, (chunk, lat_window, cols), 1)
        for d in range(domains):
            group, shift = windows_ref[d, 0] // lat_window, lax.rem(windows_ref[d, 0], lat_window)
            here = got1[k][group]
            following = got1[k][jnp.minimum(group + 1, tiles - 1)]
            rows = jnp.where(row >= shift, here.astype(F32), following.astype(F32)).astype(BF)
            found = jnp.dot(rows.reshape(chunk * lat_window, cols), pick_ref[d], preferred_element_type=F32)
            send2[k, d // 2, d % 2] = found.astype(BF).reshape(chunk, lat_window, found.shape[1])
        got2[k, region] = send2[k, region]
        for p in range(1, regions):
            second(k, p, False).start()

    def combine(k):
        for p in range(1, regions):
            second(k, p, True).wait_recv()
        total = got2[k, 0]
        for r in range(1, regions):
            total = total + got2[k, r]
        send3[k] = total
        for p in range(1, tiles):
            third(k, p, False).start()
        o_ref[pl.ds(me * share + k * chunk, chunk)] = send3[k, lax.rem(me + rotation, tiles) // half]

    o_ref[tiles * share :] = jnp.zeros_like(o_ref[tiles * share :])
    for side in range(2):
        edge(side).wait_recv()
    for k in range(chunks):
        state_rows(cuts[k], cuts[k + 1])
        for copy in leave(k):
            copy.start()
        extract(k)
        if k > 0:
            combine(k - 1)
    state_rows(cuts[chunks], rows)
    part_ref[rows + 2] = c1[...]
    skip_ref[rows + 2] = jnp.zeros(skip_ref.shape[1:], F32)
    for copy in leave(chunks):
        copy.start()
    combine(chunks - 1)
    for k in range(chunks):
        for p in range(1, tiles):
            third(k, p, True).wait_recv()
    for n in range(chunks + 1):
        for copy in leave(n):
            copy.wait()
    for side in range(2):
        edge(side).wait_send()
    for k in range(chunks):
        for p in range(1, tiles):
            first(k, p).wait_send()
            third(k, p, False).wait_send()
        for p in range(1, regions):
            second(k, p, False).wait_send()


def exchange(field, windows, state, weights, region_index, lat_window, lon_window, rotation):
    tiles, regions = lax.axis_size("tile"), lax.axis_size("region")
    channels, band, cols = field.shape
    share = -(-channels // tiles)
    chunk = 1
    chunks = share // chunk
    rows, s_ch, width = state.shape
    out, s_pad = weights.shape[0] // 4, weights.shape[1] // 3
    held = tiles * share + -(tiles * share) % 16
    col = jnp.arange(cols)[None, :, None] + region_index * cols
    pick = (col == jnp.arange(lon_window)[None, None, :] + windows[:, 2][:, None, None]).astype(BF)
    vmem = pl.BlockSpec(memory_space=pltpu.VMEM)
    block = (chunk, lat_window, lon_window)
    dma = pltpu.SemaphoreType.DMA
    return pl.pallas_call(
        functools.partial(exchange_kernel, (tiles, regions, channels, share, chunk, lat_window, rotation)),
        out_shape=(
            jax.ShapeDtypeStruct((held, lat_window, lon_window), BF),
            jax.ShapeDtypeStruct((rows + 4, out, 2 * width), F32),
            jax.ShapeDtypeStruct((rows + 4, out, width), F32),
        ),
        in_specs=[pl.BlockSpec(memory_space=pltpu.SMEM), pl.BlockSpec(memory_space=pl.ANY), vmem, vmem, vmem],
        out_specs=(vmem, pl.BlockSpec(memory_space=pl.ANY), pl.BlockSpec(memory_space=pl.ANY)),
        scratch_shapes=[
            [pltpu.VMEM((tiles, chunk, band, cols), BF)] * chunks,
            pltpu.VMEM((chunks, regions, 2) + block, BF),
            pltpu.VMEM((chunks, regions, 2) + block, BF),
            pltpu.VMEM((chunks, 2) + block, BF),
            dma((chunks, tiles)),
            dma((chunks, tiles)),
            dma((chunks,)),
            dma((chunks, regions)),
            dma((chunks, regions)),
            dma((chunks, tiles)),
            dma((chunks, tiles)),
            pltpu.VMEM((2, s_pad, width), BF),
            pltpu.VMEM((2, s_pad, width), BF),
            pltpu.VMEM((s_pad, width), BF),
            pltpu.VMEM((out, 2 * width), F32),
            pltpu.VMEM((out, 2 * width), F32),
            dma((2,)),
            dma((2,)),
            pltpu.VMEM((rows + 4, out, 2 * width), F32),
            pltpu.VMEM((rows + 4, out, width), F32),
            dma((chunks + 1,)),
            dma((chunks + 1,)),
        ],
        compiler_params=pltpu.CompilerParams(collective_id=0, has_side_effects=True, vmem_limit_bytes=44 << 20),
    )(windows, pltpu.with_memory_space_constraint(field, pltpu.HBM), pick, state, weights)


def exchange_by_collectives(field, windows, region_index, lat_window, lon_window, rotation):
    tiles, regions = lax.axis_size("tile"), lax.axis_size("region")
    pieces = windows_of_domains(field, windows, region_index, lat_window, lon_window)
    sent = pieces.reshape((regions, 2) + pieces.shape[1:])
    got = lax.all_to_all(sent, "region", split_axis=0, concat_axis=0, tiled=True)
    mine = got.astype(F32).sum(0).astype(BF)
    halves = [((t + rotation) % tiles) // (tiles // 2) for t in range(tiles)]
    spread = jnp.stack([mine[h] for h in halves])
    return lax.all_to_all(spread, "tile", split_axis=0, concat_axis=0, tiled=True)


def around(value, lanes):
    zeros = jnp.zeros(value.shape[:-1] + (lanes - value.shape[-1],), value.dtype)
    return jnp.concatenate([value[..., 2:], zeros, value[..., :2]], axis=-1)


def with_neighbours(value):
    return jnp.concatenate([pltpu.roll(value, 1, 1), value, pltpu.roll(value, value.shape[1] - 1, 1)], axis=0)


def block_kernel(step_rows, out, place, mask_ref, state_ref, cond_ref, w1_ref, b1_ref, w2_ref, b2_ref, o_ref, a1, c1, a2, c2):
    step = pl.program_id(0)

    @pl.when(step == 0)
    def _():
        for ref in (a1, c1, a2, c2):
            ref[...] = jnp.zeros_like(ref)

    width = o_ref.shape[2]
    mask = mask_ref[...] > 0
    for k in range(step_rows):
        row = jnp.concatenate([state_ref[k], cond_ref[k]], axis=0)
        d = jnp.dot(w1_ref[...], with_neighbours(row), preferred_element_type=jnp.float32)
        full = c1[...] + d[2 * out : 3 * out] + b1_ref[...]
        c1[...] = a1[...] + d[out : 2 * out]
        a1[...] = d[:out]
        y = step * step_rows + k - 3 + place[0]
        inside = mask & (y >= 0) & (y < place[1])
        hidden = jnp.where(inside, full / (1.0 + jnp.exp(-full)), 0.0).astype(BF)
        e = jnp.dot(w2_ref[...], with_neighbours(hidden), preferred_element_type=jnp.float32)
        o_ref[k] = (c2[...] + e[2 * out :] + b2_ref[...])[:, :width].astype(BF)
        c2[...] = a2[...] + e[out : 2 * out]
        a2[...] = e[:out] + d[3 * out :]


def finish_kernel(step_rows, rows, out, mask_ref, cond_ref, part_ref, skip_ref, w1_ref, b1_ref, w2_ref, b2_ref, o_ref, a1, c1, a2, c2):
    step = pl.program_id(0)

    @pl.when(step == 0)
    def _():
        for ref in (a1, c1, a2, c2):
            ref[...] = jnp.zeros_like(ref)

    width = o_ref.shape[2]
    mask = mask_ref[...] > 0
    for k in range(step_rows):
        d = jnp.dot(w1_ref[...], with_neighbours(cond_ref[k]), preferred_element_type=jnp.float32)
        full = c1[...] + d[2 * out : 3 * out] + (part_ref[k] + b1_ref[...])
        c1[...] = a1[...] + d[out : 2 * out]
        a1[...] = d[:out]
        y = step * step_rows + k - 3
        inside = mask & (y >= 0) & (y < rows)
        hidden = jnp.where(inside, full / (1.0 + jnp.exp(-full)), 0.0).astype(BF)
        near = with_neighbours(hidden)[:, :width]
        e = jnp.dot(w2_ref[...], near, preferred_element_type=jnp.float32)
        o_ref[k] = (c2[...] + e[2 * out :] + b2_ref[...]).astype(BF)
        c2[...] = a2[...] + e[out : 2 * out]
        a2[...] = e[:out] + (d[3 * out :, :width] + skip_ref[k])


def laid_out(kernel, shortcut):
    out, cin = shortcut.shape
    w = kernel.transpose(0, 2, 1, 3).reshape(3 * out, 3 * cin)
    skip = jnp.concatenate([jnp.zeros_like(shortcut), shortcut, jnp.zeros_like(shortcut)], axis=1)
    return jnp.concatenate([w, skip], axis=0)


def padded_to(w, size):
    return jnp.concatenate([w, jnp.zeros(w.shape[:-1] + (size - w.shape[-1],), w.dtype)], -1)


def of_groups(w, starts, share, size):
    parts, done = [], 0
    for start in starts:
        seen = min(max(done - start, 0), share)
        parts += [jnp.zeros(w.shape[:-1] + (seen,), w.dtype), w[..., start + seen : start + share]]
        done = max(done, start + share)
    return padded_to(jnp.concatenate(parts, -1), size)


def finish(cond, part, skip, mask, w1, first_bias, w2, second_bias, width):
    tall, lanes = cond.shape[0], cond.shape[2]
    part, skip = (pltpu.with_memory_space_constraint(v, pltpu.HBM) for v in (part, skip))
    out = part.shape[1]
    rows, step_rows = tall - 4, 4
    whole = lambda shape: pl.BlockSpec(shape, lambda i: (0,) * len(shape))
    by_row = lambda x: pl.BlockSpec((step_rows,) + x.shape[1:], lambda i: (i, 0, 0))
    total = jax.ShapeDtypeStruct((rows, out, width), BF)
    return pl.pallas_call(
        functools.partial(finish_kernel, step_rows, rows, out),
        out_shape=total,
        grid=(tall // step_rows,),
        in_specs=[whole((1, lanes)), by_row(cond), by_row(part), by_row(skip), whole(w1.shape), whole((out, 1)),
                  whole(w2.shape), whole((out, 1))],
        out_specs=pl.BlockSpec((step_rows, out, width), lambda i: (jnp.maximum(i - 1, 0), 0, 0)),
        scratch_shapes=[pltpu.VMEM((out, lanes), F32)] * 2 + [pltpu.VMEM((out, width), F32)] * 2,
        compiler_params=pltpu.CompilerParams(dimension_semantics=("arbitrary",), vmem_limit_bytes=40 << 20),
    )(mask, cond, part, skip, w1, first_bias[:, None], w2, second_bias[:, None])


def denoise(state, cond, mask, place, first_kernel, first_bias, second_kernel, second_bias, shortcut, s_ch, width, starts, share):
    tall, s_pad, lanes = state.shape
    c_pad = cond.shape[1]
    out, cin = shortcut.shape
    rows = tall - 4
    step_rows = 4

    def spread(w):
        zero = lambda n: jnp.zeros(w.shape[:-1] + (n,), w.dtype)
        parts = [w[..., :s_ch], zero(s_pad - s_ch)]
        done = s_ch
        for start in starts:
            seen = min(max(done - (s_ch + start), 0), share)
            end = s_ch + start + share
            parts += [zero(seen), w[..., end - share + seen : end]]
            done = max(done, end)
        return jnp.concatenate(parts + [zero(c_pad - share * len(starts))], -1)

    w1 = spread(first_kernel).transpose(0, 2, 1, 3).reshape(3 * out, 3 * (s_pad + c_pad))
    skip = spread(shortcut)
    skip = jnp.concatenate([jnp.zeros_like(skip), skip, jnp.zeros_like(skip)], axis=1)
    w1 = jnp.concatenate([w1, skip], axis=0)
    w2 = second_kernel.transpose(0, 2, 1, 3).reshape(3 * out, 3 * out)
    whole = lambda shape: pl.BlockSpec(shape, lambda i: (0,) * len(shape))
    total = jax.ShapeDtypeStruct((rows, out, width), BF)
    scratch = pltpu.VMEM((out, lanes), jnp.float32)
    return pl.pallas_call(
        functools.partial(block_kernel, step_rows, out),
        out_shape=total,
        grid=(tall // step_rows,),
        in_specs=[
            pl.BlockSpec(memory_space=pltpu.SMEM),
            whole((1, lanes)),
            pl.BlockSpec((step_rows, s_pad, lanes), lambda i: (i, 0, 0)),
            pl.BlockSpec((step_rows, c_pad, lanes), lambda i: (i, 0, 0)),
            whole(w1.shape),
            whole((out, 1)),
            whole(w2.shape),
            whole((out, 1)),
        ],
        out_specs=pl.BlockSpec((step_rows, out, width), lambda i: (jnp.maximum(i - 1, 0), 0, 0)),
        scratch_shapes=[scratch] * 4,
        compiler_params=pltpu.CompilerParams(dimension_semantics=("arbitrary",)),
        cost_estimate=pl.CostEstimate(
            flops=2 * tall * lanes * (w1.size + w2.size),
            bytes_accessed=2 * (state.size + cond.size + total.size),
            transcendentals=tall * out * lanes,
        ),
    )(place, mask, state, cond, w1, first_bias[:, None], w2, second_bias[:, None])


def shards(
    global_field,
    regional_state,
    windows,
    longitude_weights,
    latitude_weights,
    first_kernel,
    first_bias,
    second_kernel,
    later_conv_bias,
    shortcut_weight,
):
    tiles = lax.axis_size("tile")
    regions = lax.axis_size("region")
    tile_index = lax.axis_index("tile")
    region_index = lax.axis_index("region")
    half = tiles // 2
    row_tiles = half // TCOLS
    rotation = tiles // 4 + 2
    position = (tile_index + rotation) % tiles
    domain_half = position // half
    within = position % half
    row_tile = within // TCOLS
    col_tile = within % TCOLS
    my_domain = 2 * region_index + domain_half
    state = regional_state[0]
    channels, rows, cols = state.shape
    field_channels = global_field.shape[0]

    lat_window, lon_window = latitude_weights.shape[2], longitude_weights.shape[2]
    share = -(-field_channels // tiles)
    starts = [owned_start(t, tiles, field_channels, share) for t in range(tiles)]
    out = shortcut_weight.shape[0]
    flat = state.transpose(1, 0, 2)
    fused = global_field.shape[1] == lat_window and row_tiles == 1
    if fused:
        s_pad, c_pad = channels + -channels % 16, tiles * share + -(tiles * share) % 16
        w_state = laid_out(padded_to(first_kernel[..., :channels], s_pad), padded_to(shortcut_weight[:, :channels], s_pad))
        w_cond = laid_out(
            of_groups(first_kernel[..., channels:], starts, share, c_pad),
            of_groups(shortcut_weight[:, channels:], starts, share, c_pad),
        )
        window, part, skip = exchange(
            global_field, windows, flat, w_state, region_index, lat_window, lon_window, rotation
        )
    else:
        window = exchange_by_collectives(global_field, windows, region_index, lat_window, lon_window, rotation)
        window = window.reshape((tiles * share,) + window.shape[2:])

    own = lax.dynamic_index_in_dim(windows, my_domain, 0, keepdims=False)
    lon = lax.dynamic_index_in_dim(longitude_weights, my_domain, 0, keepdims=False)
    lon = lon * (jnp.arange(lon.shape[1]) < own[3]).astype(BF)[None, :]
    lon = lax.dynamic_slice_in_dim(jnp.pad(lon, ((2, 2), (0, 0))), col_tile * cols, cols + 4, 0)
    lat = lax.dynamic_index_in_dim(latitude_weights, domain_half, 0, keepdims=False)
    lat = lat * (jnp.arange(lat.shape[1]) < own[1]).astype(BF)[None, :]
    lat = lax.dynamic_slice_in_dim(jnp.pad(lat, ((2, 2), (0, 0))), row_tile * rows, rows + 4, 0)
    lat = jnp.roll(lat, own[0] % lat.shape[1], axis=1)

    lanes = 2 * cols
    lon = around(lon.T, lanes)
    bands = jnp.einsum("clk,kx->clx", window, lon, preferred_element_type=F32).astype(BF)
    condition = jnp.einsum("yl,clx->ycx", lat, bands, preferred_element_type=F32).astype(BF)
    x = around(jnp.arange(-2, cols + 2) + col_tile * cols + 1, lanes) - 1
    mask = ((x >= 0) & (x < TCOLS * cols)).astype(F32)[None, :]
    if fused:
        w2 = second_kernel.transpose(0, 2, 1, 3).reshape(3 * out, 3 * out)
        result = finish(condition, part, skip, mask, w_cond, first_bias, w2, later_conv_bias, cols)
        return result.transpose(1, 0, 2)[None]

    condition = jnp.pad(condition, ((0, 0), (0, -condition.shape[1] % 16), (0, 0)))
    left = passed_along(flat[:, :, cols - 2 :], "tile", 1) * (col_tile > 0).astype(BF)
    right = passed_along(flat[:, :, :2], "tile", -1) * (col_tile < TCOLS - 1).astype(BF)
    wide = around(jnp.concatenate([left, flat, right], axis=2), lanes)
    if row_tiles > 1:
        above = passed_along(wide[rows - 2 :], "tile", TCOLS) * (row_tile > 0).astype(BF)
        below = passed_along(wide[:2], "tile", -TCOLS) * (row_tile < row_tiles - 1).astype(BF)
        wide = jnp.concatenate([above, wide, below], axis=0)
        wide = jnp.pad(wide, ((0, 0), (0, -channels % 16), (0, 0)))
    else:
        wide = jnp.pad(wide, ((2, 2), (0, -channels % 16), (0, 0)))

    place = jnp.stack([row_tile * rows, row_tiles * rows]).astype(jnp.int32)
    result = denoise(
        wide, condition, mask, place, first_kernel, first_bias, second_kernel, later_conv_bias, shortcut_weight,
        channels, cols, starts, share,
    )
    return result.transpose(1, 0, 2)[None]


def solution(mesh):
    placed = (
        P(None, "tile", "region"),
        P(("region", "tile"), None, None, None),
        P(),
        P(),
        P("region", None, None),
        P(),
        P(),
        P(),
        P(),
        P(),
    )
    return jax.shard_map(
        shards,
        mesh=mesh,
        in_specs=placed,
        out_specs=P(("region", "tile"), None, None, None),
        check_vma=False,
    )
```
